128 devices in a mesh: gx: 8 (over x, core), gy: 16 (over y, z).
Axes of the slice: x: 4, y: 4, z: 4, core: 2. Of those that a mesh axis runs over, the one named last changes fastest.
Arguments:
- margin_dev: float32 [8, 16, 9, 128, 128], P('gx', 'gy'), may hold values from -0.118585412 to 0.118585412
- hamiltonian: bfloat16 [8, 16, 9, 128, 128], P('gx', 'gy'), may hold values from -0.237170825 to 0.237170825
- slot_codes: int32 [8, 16, 5], P('gx', 'gy'), may hold values from 0 to 8, as said below
- slot_count: int32 [8, 16], P('gx', 'gy'), may hold values from 3 to 5
Outputs:
- inverse_columns: float32 [8, 16, 9, 128, 128], P('gx', 'gy')
- density_columns: float32 [8, 16, 9, 128, 128], P('gx', 'gy')
The draws below stay inside these ranges and needn't reach their ends.
Inputs may be any that keep to these rules, and one draw needn't show every extreme that they name: `slot_codes`: slot 0 of every domain holds 4 (the domain itself); the other slots hold distinct codes of the eight neighbours; slots from slot_count on are unused.
All inputs are finite; a program needn't handle non-finite values.
Results may differ from the reference program's by a relative error of at most 0.0045.
Values may be sent and summed in bfloat16 or wider, within the bound.
A program may use at most 64 MiB of HBM per device.

```python
import jax
import jax.numpy as jnp
from jax import lax

B = 128
SLOTS = 5
NEWTON = 4
SIGN = 4
NBX = 8
NBY = 16


def symmetric_blocks(key, scale):
    shape = (NBX, NBY, 9, B, B)
    sample = jnp.clip(jax.random.normal(key, shape, jnp.float32), -4.0, 4.0)
    mirrored = []
    for column in range(9):
        shift_x = column // 3 - 1
        shift_y = column % 3 - 1
        moved = jnp.roll(sample[:, :, 8 - column], (-shift_x, -shift_y), axis=(0, 1))
        mirrored.append(jnp.swapaxes(moved, -1, -2))
    mirror = jnp.stack(mirrored, axis=2)
    return (sample + mirror) * (scale / 2.0 ** 0.5)


def draw_margin_dev(key, part):
    scale = 0.5 / (SLOTS * B) ** 0.5
    return symmetric_blocks(jax.random.fold_in(key, 31), scale).astype(jnp.float32)


def draw_hamiltonian(key, part):
    scale = 1.0 / (SLOTS * B) ** 0.5
    return symmetric_blocks(jax.random.fold_in(key, 37), scale).astype(jnp.bfloat16)


def draw_slot_codes(key, part):
    keys = jax.random.split(jax.random.fold_in(key, 17), NBX * NBY)
    others = jnp.array([0, 1, 2, 3, 5, 6, 7, 8], jnp.int32)
    perms = jax.vmap(lambda single: jax.random.permutation(single, others))(keys)
    selfs = jnp.full((NBX * NBY, 1), 4, jnp.int32)
    codes = jnp.concatenate([selfs, perms[:, :SLOTS - 1]], axis=1)
    return codes.reshape(NBX, NBY, SLOTS).astype(jnp.int32)


def touch_ends(values, own_key, least, largest):
    extent = values.shape
    place = [jax.random.randint(jax.random.fold_in(own_key, axis), (), 0, extent[axis]) for axis in range(len(extent))]
    values = values.at[tuple(place)].set(least)
    longest = extent.index(max(extent))
    place[longest] = (place[longest] + 1) % extent[longest]
    return values.at[tuple(place)].set(largest)


def setup_inputs(seed: int = 0) -> dict:
    key_of = jax.random.split(jax.random.key(seed), 5)
    return {
        "margin_dev": draw_margin_dev(jax.random.fold_in(key_of[4], 71), 0),
        "hamiltonian": draw_hamiltonian(jax.random.fold_in(key_of[4], 71), 0),
        "slot_codes": draw_slot_codes(jax.random.fold_in(key_of[4], 71), 0),
        "slot_count": touch_ends(jax.random.randint(key_of[3], (NBX, NBY), 3, SLOTS + 1), jax.random.fold_in(key_of[3], 1), 3, SLOTS).astype(jnp.int32),
    }


def block_indices(codes, count, slots):
    shift_x = codes // 3 - 1
    shift_y = codes % 3 - 1
    rel_x = shift_x[:, None] - shift_x[None, :]
    rel_y = shift_y[:, None] - shift_y[None, :]
    live = jnp.arange(slots, dtype=jnp.int32) < count
    valid = (jnp.abs(rel_x) <= 1) & (jnp.abs(rel_y) <= 1) & live[:, None] & live[None, :]
    stored = (rel_x + 1) * 3 + rel_y + 1
    flat_index = codes[None, :] * 9 + jnp.where(valid, stored, 0)
    return (flat_index.astype(jnp.int32), valid, live)

def build_sub(fetched, codes, count):
    slots = codes.shape[0]
    width = fetched.shape[-1]
    flat = fetched.reshape(81, width, width)
    flat_index, valid, live = block_indices(codes, count, slots)
    blocks = flat[flat_index] * valid[:, :, None, None].astype(fetched.dtype)
    return blocks.transpose(0, 2, 1, 3).reshape(slots * width, slots * width)

def place_columns(matrix, codes, count, self_term):
    slots = codes.shape[0]
    width = matrix.shape[0] // slots
    blocks = matrix.reshape(slots, width, slots, width)[:, :, 0, :]
    ident = jnp.eye(width, dtype=jnp.float32)
    first = (jnp.arange(slots) == 0).astype(jnp.float32)
    blocks = self_term[0] * first[:, None, None] * ident[None] + self_term[1] * blocks
    live = (jnp.arange(slots, dtype=jnp.int32) < count).astype(jnp.float32)
    onehot = (codes[:, None] == jnp.arange(9, dtype=jnp.int32)[None, :]).astype(jnp.float32) * live[:, None]
    return jnp.einsum('pc,pij->cij', onehot, blocks, precision=lax.Precision.HIGHEST)

def neighbours(stored, index):
    ux = index // NBY
    vy = index % NBY
    rows = (ux + jnp.arange(3, dtype=jnp.int32) - 1) % NBX
    cols = (vy + jnp.arange(3, dtype=jnp.int32) - 1) % NBY
    return stored[rows[:, None], cols[None, :]]

def reference(margin_dev, hamiltonian, slot_codes, slot_count):
    codes_flat = slot_codes.reshape(NBX * NBY, SLOTS)
    count_flat = slot_count.reshape(NBX * NBY)
    order = SLOTS * B
    hp = lax.Precision.HIGHEST

    def first_phase(index):
        codes = codes_flat[index]
        count = count_flat[index]
        sub = jnp.eye(order, dtype=jnp.float32) + build_sub(neighbours(margin_dev, index), codes, count)
        inv = jnp.eye(order, dtype=jnp.float32)
        for step in range(NEWTON):
            inv = 2.0 * inv - jnp.dot(inv, jnp.dot(sub, inv, precision=hp), precision=hp)
        return place_columns(inv, codes, count, (0.0, 1.0))
    inverse = lax.map(first_phase, jnp.arange(NBX * NBY, dtype=jnp.int32))
    inverse = inverse.reshape(NBX, NBY, 9, B, B)
    wire = inverse.astype(jnp.bfloat16)

    def second_phase(index):
        codes = codes_flat[index]
        count = count_flat[index]
        inv_sub = build_sub(neighbours(wire, index), codes, count)
        ham_sub = build_sub(neighbours(hamiltonian, index), codes, count)
        prod = jnp.dot(inv_sub, ham_sub, preferred_element_type=jnp.float32)
        sign = prod / (3.0 * jnp.sqrt(jnp.sum(prod * prod) / order) + 1e-06)
        for step in range(SIGN):
            half = sign.astype(jnp.bfloat16)
            square = jnp.dot(half, half, preferred_element_type=jnp.float32).astype(jnp.bfloat16)
            sign = 1.5 * sign - 0.5 * jnp.dot(half, square, preferred_element_type=jnp.float32)
        return place_columns(sign, codes, count, (0.5, -0.5))
    density = lax.map(second_phase, jnp.arange(NBX * NBY, dtype=jnp.int32))
    return (inverse, density.reshape(NBX, NBY, 9, B, B))
```

```python
import jax
import jax.numpy as jnp
from jax import lax
from jax.experimental import pallas as pl
from jax.experimental.pallas import tpu as pltpu
from jax.sharding import PartitionSpec as P

B = 128
SLOTS = 5
N = SLOTS * B
SIGN = 4
MESH = pl.DeviceIdType.MESH
F32 = jnp.float32
BF16 = jnp.bfloat16
EDGES = ((0, 1), (0, -1), (1, 0), (-1, 0))


def code(dx, dy):
    return 3 * (dx + 1) + dy + 1


def dot(a, b):
    return jnp.dot(a, b, preferred_element_type=F32)


def sl(p):
    return slice(p * B, (p + 1) * B)


def direct_list():
    out = []
    for ay in (1, -1):
        for r in (4, 7, 1):
            out.append(((0, ay), r, 1))
    for ax in (1, -1):
        out.append(((ax, 0), 3, 3))
        out.append(((ax, 0), code(ax, -1), 1))
        out.append(((ax, 0), code(ax, 1), 1))
    return out


def relay_list():
    return [((0, w), (ax, 0)) for w in (1, -1) for ax in (1, -1)]


def exchange_kernel(
    codes, counts, margin, ham,
    xs, hs, isub,
    mf, mb, mbuf, hown, hbuf, ibuf, wire, es, e2, e4, bpan,
    lsem, msend, mrecv, hsend, hrecv, isend, irecv,
):
    nu, nv = lax.axis_size("gx"), lax.axis_size("gy")
    u, v = lax.axis_index("gx"), lax.axis_index("gy")

    def dev(a):
        return (lax.rem(u + a[0] + nu, nu), lax.rem(v + a[1] + nv, nv))

    def remote(src, dst, send, recv, a):
        return pltpu.make_async_remote_copy(
            src_ref=src, dst_ref=dst, send_sem=send, recv_sem=recv,
            device_id=dev(a), device_id_type=MESH,
        )

    barrier = pltpu.get_barrier_semaphore()
    for a in EDGES:
        pl.semaphore_signal(barrier, inc=1, device_id=dev(a), device_id_type=MESH)

    loads = [
        pltpu.make_async_copy(
            margin.at[0, 0, pl.ds(3 * i, 3)], mf.at[pl.ds(3 * i, 3)], lsem.at[i]
        )
        for i in (1, 0, 2)
    ]
    for copy in loads:
        copy.start()
    own = pltpu.make_async_copy(ham.at[0, 0], hown.at[pl.ds(0, 9)], lsem.at[3])
    own.start()

    zero = jnp.zeros((B, B), BF16)
    mb[9] = zero
    hown[9] = zero
    wire[9] = zero
    mbuf[81] = zero
    hbuf[81] = zero
    ibuf[81] = zero
    xs[SLOTS] = jnp.zeros((B, B), F32)

    cd = [codes[0, 0, p] for p in range(SLOTS)]
    live = [p < counts[0, 0] for p in range(SLOTS)]
    ox = [c // 3 - 1 for c in cd]
    oy = [c % 3 - 1 for c in cd]

    def pair(p, q):
        rx, ry = ox[p] - ox[q], oy[p] - oy[q]
        ok = (jnp.abs(rx) <= 1) & (jnp.abs(ry) <= 1) & live[p] & live[q]
        return ok, (rx + 1) * 3 + ry + 1

    rank = [jnp.where(ox[p] == 0, 1, jnp.where(oy[p] == 0, 2, 0)) for p in range(SLOTS)]

    for i, copy in zip((1, 0, 2), loads):
        copy.wait()
        for r in range(3 * i, 3 * i + 3):
            mb[r] = mf[r].astype(BF16)

    pl.semaphore_wait(barrier, 4)

    direct, relays = direct_list(), relay_list()

    def start_direct(src, buf, send, recv):
        out = {}
        for k, (a, r, n) in enumerate(direct):
            o = code(-a[0], -a[1])
            out[(a, r)] = remote(
                src.at[pl.ds(r, n)], buf.at[pl.ds(9 * o + r, n)], send.at[k], recv.at[k], a
            )
            out[(a, r)].start()
        return out

    def start_relays(sent, buf, send, recv):
        out = []
        for w in (1, -1):
            sent[((0, -w), 4)].wait_recv()
            for ax in (1, -1):
                k = len(direct) + len(out)
                copy = remote(
                    buf.at[pl.ds(9 * code(0, w) + 4, 1)],
                    buf.at[pl.ds(9 * code(-ax, w) + 4, 1)],
                    send.at[k], recv.at[k], (ax, 0),
                )
                copy.start()
                out.append(copy)
        return out

    def wait_symmetric(sent, relayed):
        for (a, r), copy in sent.items():
            if not (a[0] == 0 and r == 4):
                copy.wait_recv()
        for copy in relayed:
            copy.wait_recv()

    def centre(dst, mine):
        for p in range(SLOTS):
            block = mine[jnp.where(live[p], cd[p], 9)]
            dst[sl(p), sl(0)] = block
            if p:
                dst[sl(0), sl(p)] = block.T

    def others(dst, buf):
        for p in range(1, SLOTS):
            dst[sl(p), sl(p)] = buf[jnp.where(live[p], cd[p] * 9 + 4, 81)]
        for p in range(1, SLOTS):
            for q in range(p + 1, SLOTS):
                ok, r = pair(p, q)
                swap = rank[p] > rank[q]
                spot = jnp.where(swap, cd[p] * 9 + 8 - r, cd[q] * 9 + r)
                block = buf[jnp.where(ok, spot, 81)].astype(F32)
                turned = block.T
                flag = jnp.where(swap, 1.0, 0.0).astype(F32)
                keep = 1.0 - flag
                dst[sl(p), sl(q)] = (keep * block + flag * turned).astype(BF16)
                dst[sl(q), sl(p)] = (keep * turned + flag * block).astype(BF16)

    msent = start_direct(mb, mbuf, msend, mrecv)
    hsent = start_direct(ham.at[0, 0], hbuf, hsend, hrecv)
    centre(es, mb)
    mrelay = start_relays(msent, mbuf, msend, mrecv)
    wait_symmetric(msent, mrelay)
    others(es, mbuf)
    hrelay = start_relays(hsent, hbuf, hsend, hrecv)

    square = dot(es[...], es[...])
    e2[...] = square.astype(BF16)
    rows = lax.broadcasted_iota(jnp.int32, (N, B), 0)
    cols = lax.broadcasted_iota(jnp.int32, (N, B), 1)
    ident = jnp.where(rows == cols, 1.0, 0.0).astype(F32)
    bpan[...] = ident - es[:, :B].astype(F32) + square[:, :B]
    e4[...] = dot(e2[...], e2[...]).astype(BF16)
    total = bpan[...] - dot(es[...], e2[:, :B])
    term = total.astype(BF16)
    for step in range(3):
        image = dot(e4[...], term)
        total = total + image
        term = image.astype(BF16)
    for p in range(SLOTS):
        xs[p] = total[sl(p), :]

    for c in range(9):
        spot = jnp.int32(SLOTS)
        for p in range(SLOTS):
            spot = jnp.where(live[p] & (cd[p] == c), p, spot)
        wire[c] = xs[spot].astype(BF16)

    zsent, xsent, relayed = {}, [], []
    k = 0
    for rx in (0, 1, -1):
        for ay in (1, -1):
            first = 3 * (rx + 1) + (1 if ay == 1 else 0)
            copy = remote(
                wire.at[pl.ds(first, 2)], ibuf.at[pl.ds(9 * code(0, -ay) + first, 2)],
                isend.at[k], irecv.at[k], (0, ay),
            )
            copy.start()
            zsent[(rx, ay)] = copy
            k += 1
    for ax in (1, -1):
        first = 3 if ax == 1 else 0
        copy = remote(
            wire.at[pl.ds(first, 6)], ibuf.at[pl.ds(9 * code(-ax, 0) + first, 6)],
            isend.at[k], irecv.at[k], (ax, 0),
        )
        copy.start()
        xsent.append(copy)
        k += 1

    own.wait()
    centre(hs, hown)
    wait_symmetric(hsent, hrelay)

    for rx in (0, 1, -1):
        for w in (1, -1):
            zsent[(rx, -w)].wait_recv()
            first = 3 * (rx + 1) + (1 if w == -1 else 0)
            for ax in ((1, -1) if rx == 0 else (rx,)):
                copy = remote(
                    ibuf.at[pl.ds(9 * code(0, w) + first, 2)],
                    ibuf.at[pl.ds(9 * code(-ax, w) + first, 2)],
                    isend.at[k], irecv.at[k], (ax, 0),
                )
                copy.start()
                relayed.append(copy)
                k += 1

    others(hs, hbuf)
    for p in range(SLOTS):
        isub[sl(p), sl(0)] = wire[jnp.where(live[p], cd[p], 9)]
    for copy in xsent + relayed:
        copy.wait_recv()
    for q in range(1, SLOTS):
        for p in range(SLOTS):
            ok, r = pair(p, q)
            isub[sl(p), sl(q)] = ibuf[jnp.where(ok, cd[q] * 9 + r, 81)]

    for copy in list(msent.values()) + mrelay + list(hsent.values()) + hrelay:
        copy.wait_send()
    for copy in list(zsent.values()) + xsent + relayed:
        copy.wait_send()


def sign_kernel(codes, counts, isub, hs, xs, inv_out, den_out, s, h, q, ds, sem):
    count = counts[0, 0]

    def spot(c):
        at = jnp.int32(SLOTS)
        for p in range(SLOTS):
            at = jnp.where((p < count) & (codes[0, 0, p] == c), p, at)
        return at

    spots = [spot(c) for c in range(9)]
    inv = [
        pltpu.make_async_copy(xs.at[spots[c]], inv_out.at[0, 0, c], sem.at[c])
        for c in range(9)
    ]
    for copy in inv:
        copy.start()
    ds[SLOTS] = jnp.zeros((B, B), F32)

    s[...] = dot(isub[...], hs[...])
    norm = jnp.sum(s[...] * s[...], keepdims=True) / N
    scale = 1.0 / (3.0 * jnp.sqrt(norm) + 1e-6)
    s[...] = s[...] * scale
    h[...] = s[...].astype(BF16)
    for step in range(SIGN - 1):
        q[...] = dot(h[...], h[...]).astype(BF16)
        s[...] = 1.5 * s[...] - 0.5 * dot(h[...], q[...])
        h[...] = s[...].astype(BF16)
    q[:, :B] = dot(h[...], h[:, :B]).astype(BF16)
    last = 1.5 * s[:, :B] - 0.5 * dot(h[...], q[:, :B])
    rows = lax.broadcasted_iota(jnp.int32, (B, B), 0)
    cols = lax.broadcasted_iota(jnp.int32, (B, B), 1)
    ident = jnp.where(rows == cols, 0.5, 0.0).astype(F32)
    for p in range(SLOTS):
        block = -0.5 * last[sl(p), :]
        ds[p] = block + ident if p == 0 else block
    den = [
        pltpu.make_async_copy(ds.at[spots[c]], den_out.at[0, 0, c], sem.at[9 + c])
        for c in range(9)
    ]
    for copy in den:
        copy.start()
    for copy in inv + den:
        copy.wait()


def local(margin_dev, hamiltonian, slot_codes, slot_count):
    vm = pl.BlockSpec(memory_space=pltpu.VMEM)
    sm = pl.BlockSpec(memory_space=pltpu.SMEM)
    hbm = pl.BlockSpec(memory_space=pltpu.HBM)
    shape = jax.ShapeDtypeStruct
    n_sym = len(direct_list()) + len(relay_list())
    dma = pltpu.SemaphoreType.DMA
    xs, hs, isub = pl.pallas_call(
        exchange_kernel,
        out_shape=(
            shape((SLOTS + 1, B, B), F32),
            shape((N, N), BF16),
            shape((N, N), BF16),
        ),
        in_specs=[sm, sm, hbm, hbm],
        out_specs=(vm, vm, vm),
        scratch_shapes=[
            pltpu.VMEM((9, B, B), F32),
            pltpu.VMEM((10, B, B), BF16),
            pltpu.VMEM((82, B, B), BF16),
            pltpu.VMEM((10, B, B), BF16),
            pltpu.VMEM((82, B, B), BF16),
            pltpu.VMEM((82, B, B), BF16),
            pltpu.VMEM((10, B, B), BF16),
            pltpu.VMEM((N, N), BF16),
            pltpu.VMEM((N, N), BF16),
            pltpu.VMEM((N, N), BF16),
            pltpu.VMEM((N, B), F32),
            dma((4,)),
            dma((n_sym,)),
            dma((n_sym,)),
            dma((n_sym,)),
            dma((n_sym,)),
            dma((16,)),
            dma((16,)),
        ],
        compiler_params=pltpu.CompilerParams(
            collective_id=0, has_side_effects=True, vmem_limit_bytes=32 << 20
        ),
        name="exchange",
    )(slot_codes, slot_count, margin_dev, hamiltonian)
    return pl.pallas_call(
        sign_kernel,
        out_shape=(
            shape((1, 1, 9, B, B), F32),
            shape((1, 1, 9, B, B), F32),
        ),
        in_specs=[sm, sm, vm, vm, vm],
        out_specs=(hbm, hbm),
        scratch_shapes=[
            pltpu.VMEM((N, N), F32),
            pltpu.VMEM((N, N), BF16),
            pltpu.VMEM((N, N), BF16),
            pltpu.VMEM((SLOTS + 1, B, B), F32),
            dma((18,)),
        ],
        compiler_params=pltpu.CompilerParams(vmem_limit_bytes=32 << 20),
        name="sign",
    )(slot_codes, slot_count, isub, hs, xs)


def solution(mesh):
    return jax.shard_map(
        local,
        mesh=mesh,
        in_specs=(
            P("gx", "gy", None, None, None),
            P("gx", "gy", None, None, None),
            P("gx", "gy", None),
            P("gx", "gy"),
        ),
        out_specs=(P("gx", "gy", None, None, None), P("gx", "gy", None, None, None)),
        check_vma=False,
    )
```

```python
import jax
import jax.numpy as jnp
from jax import lax
from jax.experimental import pallas as pl
from jax.experimental.pallas import tpu as pltpu
from jax.sharding import PartitionSpec as P

B = 128
SLOTS = 5
N = SLOTS * B
SIGN = 4
MESH = pl.DeviceIdType.MESH
F32 = jnp.float32
BF16 = jnp.bfloat16
EDGES = ((0, 1), (0, -1), (1, 0), (-1, 0))


def code(dx, dy):
    return 3 * (dx + 1) + dy + 1


def dot(a, b):
    return jnp.dot(a, b, preferred_element_type=F32)


def sl(p):
    return slice(p * B, (p + 1) * B)


def direct_list():
    out = []
    for ay in (1, -1):
        for r in (4, 7, 1):
            out.append(((0, ay), r, 1))
    for ax in (1, -1):
        out.append(((ax, 0), 3, 3))
        out.append(((ax, 0), code(ax, -1), 1))
        out.append(((ax, 0), code(ax, 1), 1))
    return out


def relay_list():
    return [((0, w), (ax, 0)) for w in (1, -1) for ax in (1, -1)]


def exchange_kernel(
    codes, counts, margin, ham,
    xs, hs, isub,
    mf, mb, mbuf, hown, hbuf, ibuf, wire, es, e2, e4, bpan,
    lsem, msend, mrecv, hsend, hrecv, isend, irecv,
):
    nu, nv = lax.axis_size("gx"), lax.axis_size("gy")
    u, v = lax.axis_index("gx"), lax.axis_index("gy")

    def dev(a):
        return (lax.rem(u + a[0] + nu, nu), lax.rem(v + a[1] + nv, nv))

    def remote(src, dst, send, recv, a):
        return pltpu.make_async_remote_copy(
            src_ref=src, dst_ref=dst, send_sem=send, recv_sem=recv,
            device_id=dev(a), device_id_type=MESH,
        )

    barrier = pltpu.get_barrier_semaphore()
    for a in EDGES:
        pl.semaphore_signal(barrier, inc=1, device_id=dev(a), device_id_type=MESH)

    loads = [
        pltpu.make_async_copy(
            margin.at[0, 0, pl.ds(3 * i, 3)], mf.at[pl.ds(3 * i, 3)], lsem.at[i]
        )
        for i in (1, 0, 2)
    ]
    for copy in loads:
        copy.start()
    own = pltpu.make_async_copy(ham.at[0, 0], hown.at[pl.ds(0, 9)], lsem.at[3])
    own.start()

    zero = jnp.zeros((B, B), BF16)
    mb[9] = zero
    hown[9] = zero
    wire[9] = zero
    mbuf[81] = zero
    hbuf[81] = zero
    ibuf[81] = zero
    xs[SLOTS] = jnp.zeros((B, B), F32)

    cd = [codes[0, 0, p] for p in range(SLOTS)]
    live = [p < counts[0, 0] for p in range(SLOTS)]
    ox = [c // 3 - 1 for c in cd]
    oy = [c % 3 - 1 for c in cd]

    def pair(p, q):
        rx, ry = ox[p] - ox[q], oy[p] - oy[q]
        ok = (jnp.abs(rx) <= 1) & (jnp.abs(ry) <= 1) & live[p] & live[q]
        return ok, (rx + 1) * 3 + ry + 1

    rank = [jnp.where(ox[p] == 0, 1, jnp.where(oy[p] == 0, 2, 0)) for p in range(SLOTS)]

    for i, copy in zip((1, 0, 2), loads):
        copy.wait()
        for r in range(3 * i, 3 * i + 3):
            mb[r] = mf[r].astype(BF16)

    pl.semaphore_wait(barrier, 4)

    direct, relays = direct_list(), relay_list()

    def start_direct(src, buf, send, recv):
        out = {}
        for k, (a, r, n) in enumerate(direct):
            o = code(-a[0], -a[1])
            out[(a, r)] = remote(
                src.at[pl.ds(r, n)], buf.at[pl.ds(9 * o + r, n)], send.at[k], recv.at[k], a
            )
            out[(a, r)].start()
        return out

    def start_relays(sent, buf, send, recv):
        out = []
        for w in (1, -1):
            sent[((0, -w), 4)].wait_recv()
            for ax in (1, -1):
                k = len(direct) + len(out)
                copy = remote(
                    buf.at[pl.ds(9 * code(0, w) + 4, 1)],
                    buf.at[pl.ds(9 * code(-ax, w) + 4, 1)],
                    send.at[k], recv.at[k], (ax, 0),
                )
                copy.start()
                out.append(copy)
        return out

    def wait_symmetric(sent, relayed):
        for (a, r), copy in sent.items():
            if not (a[0] == 0 and r == 4):
                copy.wait_recv()
        for copy in relayed:
            copy.wait_recv()

    def centre(dst, mine):
        for p in range(SLOTS):
            block = mine[jnp.where(live[p], cd[p], 9)]
            dst[sl(p), sl(0)] = block
            if p:
                dst[sl(0), sl(p)] = block.T

    def others(dst, buf):
        for p in range(1, SLOTS):
            dst[sl(p), sl(p)] = buf[jnp.where(live[p], cd[p] * 9 + 4, 81)]
        for p in range(1, SLOTS):
            for q in range(p + 1, SLOTS):
                ok, r = pair(p, q)
                swap = rank[p] > rank[q]
                spot = jnp.where(swap, cd[p] * 9 + 8 - r, cd[q] * 9 + r)
                block = buf[jnp.where(ok, spot, 81)].astype(F32)
                turned = block.T
                flag = jnp.where(swap, 1.0, 0.0).astype(F32)
                keep = 1.0 - flag
                dst[sl(p), sl(q)] = (keep * block + flag * turned).astype(BF16)
                dst[sl(q), sl(p)] = (keep * turned + flag * block).astype(BF16)

    msent = start_direct(mb, mbuf, msend, mrecv)
    hsent = start_direct(ham.at[0, 0], hbuf, hsend, hrecv)
    centre(es, mb)
    mrelay = start_relays(msent, mbuf, msend, mrecv)
    wait_symmetric(msent, mrelay)
    others(es, mbuf)
    hrelay = start_relays(hsent, hbuf, hsend, hrecv)

    square = dot(es[...], es[...])
    e2[...] = square.astype(BF16)
    rows = lax.broadcasted_iota(jnp.int32, (N, B), 0)
    cols = lax.broadcasted_iota(jnp.int32, (N, B), 1)
    ident = jnp.where(rows == cols, 1.0, 0.0).astype(F32)
    bpan[...] = ident - es[:, :B].astype(F32) + square[:, :B]
    e4[...] = dot(e2[...], e2[...]).astype(BF16)
    total = bpan[...] - dot(es[...], e2[:, :B])
    term = total.astype(BF16)
    for step in range(3):
        image = dot(e4[...], term)
        total = total + image
        term = image.astype(BF16)
    for p in range(SLOTS):
        xs[p] = total[sl(p), :]

    for c in range(9):
        spot = jnp.int32(SLOTS)
        for p in range(SLOTS):
            spot = jnp.where(live[p] & (cd[p] == c), p, spot)
        wire[c] = xs[spot].astype(BF16)

    zsent, xsent, relayed = {}, [], []
    k = 0
    for rx in (0, 1, -1):
        for ay in (1, -1):
            first = 3 * (rx + 1) + (1 if ay == 1 else 0)
            copy = remote(
                wire.at[pl.ds(first, 2)], ibuf.at[pl.ds(9 * code(0, -ay) + first, 2)],
                isend.at[k], irecv.at[k], (0, ay),
            )
            copy.start()
            zsent[(rx, ay)] = copy
            k += 1
    for ax in (1, -1):
        first = 3 if ax == 1 else 0
        copy = remote(
            wire.at[pl.ds(first, 6)], ibuf.at[pl.ds(9 * code(-ax, 0) + first, 6)],
            isend.at[k], irecv.at[k], (ax, 0),
        )
        copy.start()
        xsent.append(copy)
        k += 1

    own.wait()
    centre(hs, hown)
    wait_symmetric(hsent, hrelay)

    for rx in (0, 1, -1):
        for w in (1, -1):
            zsent[(rx, -w)].wait_recv()
            first = 3 * (rx + 1) + (1 if w == -1 else 0)
            for ax in ((1, -1) if rx == 0 else (rx,)):
                copy = remote(
                    ibuf.at[pl.ds(9 * code(0, w) + first, 2)],
                    ibuf.at[pl.ds(9 * code(-ax, w) + first, 2)],
                    isend.at[k], irecv.at[k], (ax, 0),
                )
                copy.start()
                relayed.append(copy)
                k += 1

    others(hs, hbuf)
    for p in range(SLOTS):
        isub[sl(p), sl(0)] = wire[jnp.where(live[p], cd[p], 9)]
    for copy in xsent + relayed:
        copy.wait_recv()
    for q in range(1, SLOTS):
        for p in range(SLOTS):
            ok, r = pair(p, q)
            isub[sl(p), sl(q)] = ibuf[jnp.where(ok, cd[q] * 9 + r, 81)]

    for copy in list(msent.values()) + mrelay + list(hsent.values()) + hrelay:
        copy.wait_send()
    for copy in list(zsent.values()) + xsent + relayed:
        copy.wait_send()


def sign_kernel(codes, counts, isub, hs, xs, inv_out, den_out, s, h, q, ds, sem):
    count = counts[0, 0]

    def spot(c):
        at = jnp.int32(SLOTS)
        for p in range(SLOTS):
            at = jnp.where((p < count) & (codes[0, 0, p] == c), p, at)
        return at

    spots = [spot(c) for c in range(9)]
    inv = [
        pltpu.make_async_copy(xs.at[spots[c]], inv_out.at[0, 0, c], sem.at[c])
        for c in range(9)
    ]
    for copy in inv:
        copy.start()
    ds[SLOTS] = jnp.zeros((B, B), F32)

    s[...] = dot(isub[...], hs[...])
    norm = jnp.sum(s[...] * s[...], keepdims=True) / N
    scale = 1.0 / (3.0 * jnp.sqrt(norm) + 1e-6)
    s[...] = s[...] * scale
    h[...] = s[...].astype(BF16)
    for step in range(SIGN - 1):
        q[...] = dot(h[...], h[...]).astype(BF16)
        s[...] = 1.5 * s[...] - 0.5 * dot(h[...], q[...])
        h[...] = s[...].astype(BF16)
    q[:, :B] = dot(h[...], h[:, :B]).astype(BF16)
    last = 1.5 * s[:, :B] - 0.5 * dot(h[...], q[:, :B])
    rows = lax.broadcasted_iota(jnp.int32, (B, B), 0)
    cols = lax.broadcasted_iota(jnp.int32, (B, B), 1)
    ident = jnp.where(rows == cols, 0.5, 0.0).astype(F32)
    for p in range(SLOTS):
        block = -0.5 * last[sl(p), :]
        ds[p] = block + ident if p == 0 else block
    den = [
        pltpu.make_async_copy(ds.at[spots[c]], den_out.at[0, 0, c], sem.at[9 + c])
        for c in range(9)
    ]
    for copy in den:
        copy.start()
    for copy in inv + den:
        copy.wait()


def local(margin_dev, hamiltonian, slot_codes, slot_count):
    vm = pl.BlockSpec(memory_space=pltpu.VMEM)
    sm = pl.BlockSpec(memory_space=pltpu.SMEM)
    hbm = pl.BlockSpec(memory_space=pltpu.HBM)
    shape = jax.ShapeDtypeStruct
    n_sym = len(direct_list()) + len(relay_list())
    dma = pltpu.SemaphoreType.DMA
    xs, hs, isub = pl.pallas_call(
        exchange_kernel,
        out_shape=(
            shape((SLOTS + 1, B, B), F32),
            shape((N, N), BF16),
            shape((N, N), BF16),
        ),
        in_specs=[sm, sm, hbm, hbm],
        out_specs=(vm, vm, vm),
        scratch_shapes=[
            pltpu.VMEM((9, B, B), F32),
            pltpu.VMEM((10, B, B), BF16),
            pltpu.VMEM((82, B, B), BF16),
            pltpu.VMEM((10, B, B), BF16),
            pltpu.VMEM((82, B, B), BF16),
            pltpu.VMEM((82, B, B), BF16),
            pltpu.VMEM((10, B, B), BF16),
            pltpu.VMEM((N, N), BF16),
            pltpu.VMEM((N, N), BF16),
            pltpu.VMEM((N, N), BF16),
            pltpu.VMEM((N, B), F32),
            dma((4,)),
            dma((n_sym,)),
            dma((n_sym,)),
            dma((n_sym,)),
            dma((n_sym,)),
            dma((16,)),
            dma((16,)),
        ],
        compiler_params=pltpu.CompilerParams(
            collective_id=0, has_side_effects=True, vmem_limit_bytes=32 << 20
        ),
        name="exchange",
    )(
        slot_codes,
        slot_count,
        pltpu.with_memory_space_constraint(margin_dev, pltpu.HBM),
        pltpu.with_memory_space_constraint(hamiltonian, pltpu.HBM),
    )
    return pl.pallas_call(
        sign_kernel,
        out_shape=(
            shape((1, 1, 9, B, B), F32),
            shape((1, 1, 9, B, B), F32),
        ),
        in_specs=[sm, sm, vm, vm, vm],
        out_specs=(hbm, hbm),
        scratch_shapes=[
            pltpu.VMEM((N, N), F32),
            pltpu.VMEM((N, N), BF16),
            pltpu.VMEM((N, N), BF16),
            pltpu.VMEM((SLOTS + 1, B, B), F32),
            dma((18,)),
        ],
        compiler_params=pltpu.CompilerParams(vmem_limit_bytes=32 << 20),
        name="sign",
    )(slot_codes, slot_count, isub, hs, xs)


def solution(mesh):
    return jax.shard_map(
        local,
        mesh=mesh,
        in_specs=(
            P("gx", "gy", None, None, None),
            P("gx", "gy", None, None, None),
            P("gx", "gy", None),
            P("gx", "gy"),
        ),
        out_specs=(P("gx", "gy", None, None, None), P("gx", "gy", None, None, None)),
        check_vma=False,
    )
```

```python
import jax
import jax.numpy as jnp
from jax import lax
from jax.experimental import pallas as pl
from jax.experimental.pallas import tpu as pltpu
from jax.sharding import PartitionSpec as P

B = 128
SLOTS = 5
N = SLOTS * B
SIGN = 4
MESH = pl.DeviceIdType.MESH
F32 = jnp.float32
BF16 = jnp.bfloat16
EDGES = ((0, 1), (0, -1), (1, 0), (-1, 0))


def code(dx, dy):
    return 3 * (dx + 1) + dy + 1


def dot(a, b):
    return jnp.dot(a, b, preferred_element_type=F32)


def sl(p):
    return slice(p * B, (p + 1) * B)


def rows_of(step):
    return 3 * (step + 1)


def exchange_kernel(
    codes_hbm, counts, margin, ham,
    xs, hs, isub,
    codes, mf, mb, mbuf, hown, hbuf, ibuf, wire, es, e2, e4,
    lsem, msend, mrecv, hsend, hrecv, isend, irecv,
):
    nu, nv = lax.axis_size("gx"), lax.axis_size("gy")
    u, v = lax.axis_index("gx"), lax.axis_index("gy")
    core = lax.rem(u, 2)
    off = 2 * core - 1
    on = -off

    def dev(a):
        return (lax.rem(u + a[0] + nu, nu), lax.rem(v + a[1] + nv, nv))

    def remote(src, dst, send, recv, a):
        return pltpu.make_async_remote_copy(
            src_ref=src, dst_ref=dst, send_sem=send, recv_sem=recv,
            device_id=dev(a), device_id_type=MESH,
        )

    barrier = pltpu.get_barrier_semaphore()
    for a in EDGES:
        pl.semaphore_signal(barrier, inc=1, device_id=dev(a), device_id_type=MESH)

    loads = [
        pltpu.make_async_copy(
            margin.at[0, 0, pl.ds(3 * i, 3)], mf.at[pl.ds(3 * i, 3)], lsem.at[i]
        )
        for i in (1, 0, 2)
    ]
    listed = pltpu.make_async_copy(codes_hbm, codes, lsem.at[4])
    own = pltpu.make_async_copy(ham.at[0, 0], hown.at[pl.ds(0, 9)], lsem.at[3])
    for copy in loads + [listed, own]:
        copy.start()

    zero = jnp.zeros((B, B), BF16)
    mb[9] = zero
    hown[9] = zero
    wire[9] = zero
    mbuf[81] = zero
    hbuf[81] = zero
    ibuf[81] = zero
    xs[SLOTS] = jnp.zeros((B, B), F32)

    for i, copy in zip((1, 0, 2), loads):
        copy.wait()
        for r in range(3 * i, 3 * i + 3):
            mb[r] = mf[r].astype(BF16)

    pl.semaphore_wait(barrier, 4)

    def start_direct(src, buf, send, recv):
        early, late = [], []
        k = 0
        for r in (4, 7, 1):
            for ay in (1, -1):
                copy = remote(
                    src.at[pl.ds(r, 1)], buf.at[pl.ds(9 * code(0, -ay) + r, 1)],
                    send.at[k], recv.at[k], (0, ay),
                )
                copy.start()
                (early if r == 4 else late).append(copy)
                k += 1
        for d in (off, on):
            for r, n in ((3, 3), (rows_of(d), 1), (rows_of(d) + 2, 1)):
                copy = remote(
                    src.at[pl.ds(r, n)], buf.at[pl.ds(9 * code(-d, 0) + r, n)],
                    send.at[k], recv.at[k], (d, 0),
                )
                copy.start()
                late.append(copy)
                k += 1
        return early, late

    def start_relays(early, buf, send, recv):
        out = []
        k = 12
        for copy in early:
            copy.wait_recv()
        for d in (off, on):
            for w in (-1, 1):
                copy = remote(
                    buf.at[pl.ds(9 * code(0, w) + 4, 1)],
                    buf.at[pl.ds(9 * code(-d, w) + 4, 1)],
                    send.at[k], recv.at[k], (d, 0),
                )
                copy.start()
                out.append(copy)
                k += 1
        return out

    msent = start_direct(mb, mbuf, msend, mrecv)
    hsent = start_direct(ham.at[0, 0], hbuf, hsend, hrecv)

    listed.wait()
    cd = [codes[0, 0, p] for p in range(SLOTS)]
    live = [p < counts[0, 0] for p in range(SLOTS)]
    ox = [c // 3 - 1 for c in cd]
    oy = [c % 3 - 1 for c in cd]

    def pair(p, q):
        rx, ry = ox[p] - ox[q], oy[p] - oy[q]
        ok = (jnp.abs(rx) <= 1) & (jnp.abs(ry) <= 1) & live[p] & live[q]
        return ok, (rx + 1) * 3 + ry + 1

    rank = [jnp.where(ox[p] == 0, 1, jnp.where(oy[p] == 0, 2, 0)) for p in range(SLOTS)]

    def centre(dst, mine):
        for p in range(SLOTS):
            block = mine[jnp.where(live[p], cd[p], 9)]
            dst[sl(p), sl(0)] = block
            if p:
                dst[sl(0), sl(p)] = block.T

    def others(dst, buf):
        for p in range(1, SLOTS):
            dst[sl(p), sl(p)] = buf[jnp.where(live[p], cd[p] * 9 + 4, 81)]
        for p in range(1, SLOTS):
            for q in range(p + 1, SLOTS):
                ok, r = pair(p, q)
                swap = rank[p] > rank[q]
                spot = jnp.where(swap, cd[p] * 9 + 8 - r, cd[q] * 9 + r)
                block = buf[jnp.where(ok, spot, 81)].astype(F32)
                turned = block.T
                flag = jnp.where(swap, 1.0, 0.0).astype(F32)
                keep = 1.0 - flag
                dst[sl(p), sl(q)] = (keep * block + flag * turned).astype(BF16)
                dst[sl(q), sl(p)] = (keep * turned + flag * block).astype(BF16)

    centre(es, mb)
    mrelay = start_relays(msent[0], mbuf, msend, mrecv)
    for copy in msent[1] + mrelay:
        copy.wait_recv()
    others(es, mbuf)
    hrelay = start_relays(hsent[0], hbuf, hsend, hrecv)

    rows = lax.broadcasted_iota(jnp.int32, (N, B), 0)
    cols = lax.broadcasted_iota(jnp.int32, (N, B), 1)
    first = jnp.where(rows == cols, 1.0, 0.0).astype(F32) - es[:, :B].astype(F32)
    e2[:, :N] = dot(es[...], es[...]).astype(BF16)
    e2[:, N:] = first.astype(BF16)
    both = dot(e2[:, :N], e2[...])
    e4[...] = both[:, :N].astype(BF16)
    total = first + both[:, N:]
    term = total.astype(BF16)
    for step in range(3):
        image = dot(e4[...], term)
        total = total + image
        term = image.astype(BF16)
    for p in range(SLOTS):
        xs[p] = total[sl(p), :]

    for c in range(9):
        spot = jnp.int32(SLOTS)
        for p in range(SLOTS):
            spot = jnp.where(live[p] & (cd[p] == c), p, spot)
        wire[c] = xs[spot].astype(BF16)

    zsent, xsent, relayed = {}, [], []
    k = 0
    for name, rx in (("mid", 0), ("off", off), ("on", on)):
        for ay in (1, -1):
            first = rows_of(rx) + (1 if ay == 1 else 0)
            copy = remote(
                wire.at[pl.ds(first, 2)], ibuf.at[pl.ds(9 * code(0, -ay) + first, 2)],
                isend.at[k], irecv.at[k], (0, ay),
            )
            copy.start()
            zsent[(name, ay)] = copy
            k += 1
    for d in (off, on):
        first = 3 * ((d + 1) // 2)
        copy = remote(
            wire.at[pl.ds(first, 6)], ibuf.at[pl.ds(9 * code(-d, 0) + first, 6)],
            isend.at[k], irecv.at[k], (d, 0),
        )
        copy.start()
        xsent.append(copy)
        k += 1

    def relay(rx, w, d, k):
        first = rows_of(rx) + (1 if w == -1 else 0)
        copy = remote(
            ibuf.at[pl.ds(9 * code(0, w) + first, 2)],
            ibuf.at[pl.ds(9 * code(-d, w) + first, 2)],
            isend.at[k], irecv.at[k], (d, 0),
        )
        copy.start()
        relayed.append(copy)

    own.wait()
    centre(hs, hown)
    for copy in hsent[1] + hrelay:
        copy.wait_recv()
    for w in (1, -1):
        zsent[("mid", -w)].wait_recv()
        relay(0, w, off, k)
        k += 1
    for w in (1, -1):
        zsent[("off", -w)].wait_recv()
        relay(off, w, off, k)
        k += 1
    for w in (1, -1):
        relay(0, w, on, k)
        k += 1
    for w in (1, -1):
        zsent[("on", -w)].wait_recv()
        relay(on, w, on, k)
        k += 1

    others(hs, hbuf)
    for p in range(SLOTS):
        isub[sl(p), sl(0)] = wire[jnp.where(live[p], cd[p], 9)]
    for copy in xsent + relayed:
        copy.wait_recv()
    for q in range(1, SLOTS):
        for p in range(SLOTS):
            ok, r = pair(p, q)
            isub[sl(p), sl(q)] = ibuf[jnp.where(ok, cd[q] * 9 + r, 81)]

    for copy in msent[0] + msent[1] + mrelay + hsent[0] + hsent[1] + hrelay:
        copy.wait_send()
    for copy in list(zsent.values()) + xsent + relayed:
        copy.wait_send()


def sign_kernel(
    codes_hbm, counts, isub, hs, xs, inv_out, den_out,
    codes, s, h, g, q, ds, sem,
):
    listed = pltpu.make_async_copy(codes_hbm, codes, sem.at[18])
    listed.start()
    ds[SLOTS] = jnp.zeros((B, B), F32)

    product = dot(isub[...], hs[...])
    s[...] = product
    h[...] = product.astype(BF16)
    norm = jnp.sum(jnp.sum(product * product, axis=0, keepdims=True), keepdims=True) / N
    scale = 1.0 / (3.0 * jnp.sqrt(norm) + 1e-6)

    listed.wait()
    count = counts[0, 0]
    spots = []
    for c in range(9):
        at = jnp.int32(SLOTS)
        for p in range(SLOTS):
            at = jnp.where((p < count) & (codes[0, 0, p] == c), p, at)
        spots.append(at)
    inv = [
        pltpu.make_async_copy(xs.at[spots[c]], inv_out.at[0, 0, c], sem.at[c])
        for c in range(9)
    ]
    for copy in inv:
        copy.start()

    a, b = h, g
    for step in range(SIGN - 1):
        square = dot(a[...], a[...])
        q[...] = (square * (scale * scale) if step == 0 else square).astype(BF16)
        new = 1.5 * s[...] - 0.5 * dot(a[...], q[...])
        if step == 0:
            new = new * scale
        s[...] = new
        b[...] = new.astype(BF16)
        a, b = b, a
    q[:, :B] = dot(a[...], a[:, :B]).astype(BF16)
    rows = lax.broadcasted_iota(jnp.int32, (B, B), 0)
    cols = lax.broadcasted_iota(jnp.int32, (B, B), 1)
    ident = jnp.where(rows == cols, 0.5, 0.0).astype(F32)
    for p in range(SLOTS):
        last = 1.5 * s[sl(p), :B] - 0.5 * dot(a[sl(p), :], q[:, :B])
        ds[p] = ident - 0.5 * last if p == 0 else -0.5 * last
    den = [
        pltpu.make_async_copy(ds.at[spots[c]], den_out.at[0, 0, c], sem.at[9 + c])
        for c in range(9)
    ]
    for copy in den:
        copy.start()
    for copy in inv + den:
        copy.wait()


def local(margin_dev, hamiltonian, slot_codes, slot_count):
    vm = pl.BlockSpec(memory_space=pltpu.VMEM)
    hbm = pl.BlockSpec(memory_space=pltpu.HBM)
    shape = jax.ShapeDtypeStruct
    dma = pltpu.SemaphoreType.DMA
    n_sym = 16
    sm = pl.BlockSpec(memory_space=pltpu.SMEM)
    slot_codes, margin_dev, hamiltonian = (
        pltpu.with_memory_space_constraint(x, pltpu.HBM)
        for x in (slot_codes, margin_dev, hamiltonian)
    )
    xs, hs, isub = pl.pallas_call(
        exchange_kernel,
        out_shape=(
            shape((SLOTS + 1, B, B), F32),
            shape((N, N), BF16),
            shape((N, N), BF16),
        ),
        in_specs=[hbm, sm, hbm, hbm],
        out_specs=(vm, vm, vm),
        scratch_shapes=[
            pltpu.SMEM((1, 1, SLOTS), jnp.int32),
            pltpu.VMEM((9, B, B), F32),
            pltpu.VMEM((10, B, B), BF16),
            pltpu.VMEM((82, B, B), BF16),
            pltpu.VMEM((10, B, B), BF16),
            pltpu.VMEM((82, B, B), BF16),
            pltpu.VMEM((82, B, B), BF16),
            pltpu.VMEM((10, B, B), BF16),
            pltpu.VMEM((N, N), BF16),
            pltpu.VMEM((N, N + B), BF16),
            pltpu.VMEM((N, N), BF16),
            dma((5,)),
            dma((n_sym,)),
            dma((n_sym,)),
            dma((n_sym,)),
            dma((n_sym,)),
            dma((16,)),
            dma((16,)),
        ],
        compiler_params=pltpu.CompilerParams(
            collective_id=0, has_side_effects=True, vmem_limit_bytes=32 << 20
        ),
        name="exchange",
    )(slot_codes, slot_count, margin_dev, hamiltonian)
    return pl.pallas_call(
        sign_kernel,
        out_shape=(
            shape((1, 1, 9, B, B), F32),
            shape((1, 1, 9, B, B), F32),
        ),
        in_specs=[hbm, sm, vm, vm, vm],
        out_specs=(hbm, hbm),
        scratch_shapes=[
            pltpu.SMEM((1, 1, SLOTS), jnp.int32),
            pltpu.VMEM((N, N), F32),
            pltpu.VMEM((N, N), BF16),
            pltpu.VMEM((N, N), BF16),
            pltpu.VMEM((N, N), BF16),
            pltpu.VMEM((SLOTS + 1, B, B), F32),
            dma((19,)),
        ],
        compiler_params=pltpu.CompilerParams(vmem_limit_bytes=32 << 20),
        name="sign",
    )(slot_codes, slot_count, isub, hs, xs)


def solution(mesh):
    return jax.shard_map(
        local,
        mesh=mesh,
        in_specs=(
            P("gx", "gy", None, None, None),
            P("gx", "gy", None, None, None),
            P("gx", "gy", None),
            P("gx", "gy"),
        ),
        out_specs=(P("gx", "gy", None, None, None), P("gx", "gy", None, None, None)),
        check_vma=False,
    )
```

```python
import jax
import jax.numpy as jnp
from jax import lax
from jax.experimental import pallas as pl
from jax.experimental.pallas import tpu as pltpu
from jax.sharding import PartitionSpec as P

B = 128
SLOTS = 5
N = SLOTS * B
SIGN = 4
MESH = pl.DeviceIdType.MESH
F32 = jnp.float32
BF16 = jnp.bfloat16
EDGES = ((0, 1), (0, -1), (1, 0), (-1, 0))


def code(dx, dy):
    return 3 * (dx + 1) + dy + 1


def dot(a, b):
    return jnp.dot(a, b, preferred_element_type=F32)


def sl(p):
    return slice(p * B, (p + 1) * B)


def rows_of(step):
    return 3 * (step + 1)


def exchange_kernel(
    codes_hbm, counts, margin, ham,
    xs, hs, isub,
    codes, mf, mb, mbuf, mdiag, hown, hbuf, hdiag, ibuf, wire, es, e2, e4,
    lsem, msend, mrecv, hsend, hrecv, isend, irecv,
):
    nu, nv = lax.axis_size("gx"), lax.axis_size("gy")
    u, v = lax.axis_index("gx"), lax.axis_index("gy")
    core = lax.rem(u, 2)
    off = 2 * core - 1
    on = -off

    def dev(a):
        return (lax.rem(u + a[0] + nu, nu), lax.rem(v + a[1] + nv, nv))

    def remote(src, dst, send, recv, a):
        return pltpu.make_async_remote_copy(
            src_ref=src, dst_ref=dst, send_sem=send, recv_sem=recv,
            device_id=dev(a), device_id_type=MESH,
        )

    barrier = pltpu.get_barrier_semaphore()
    for a in EDGES:
        pl.semaphore_signal(barrier, inc=1, device_id=dev(a), device_id_type=MESH)

    loads = [
        pltpu.make_async_copy(
            margin.at[0, 0, pl.ds(3 * i, 3)], mf.at[pl.ds(3 * i, 3)], lsem.at[i]
        )
        for i in (1, 0, 2)
    ]
    listed = pltpu.make_async_copy(codes_hbm, codes, lsem.at[4])
    own = pltpu.make_async_copy(ham.at[0, 0], hown.at[pl.ds(0, 9)], lsem.at[3])
    for copy in loads + [listed, own]:
        copy.start()

    zero = jnp.zeros((B, B), BF16)
    mb[9] = zero
    hown[9] = zero
    wire[9] = zero
    mbuf[81] = zero
    hbuf[81] = zero
    mdiag[9] = zero
    hdiag[9] = zero
    ibuf[81] = zero
    xs[SLOTS] = jnp.zeros((B, B), F32)

    for i, copy in zip((1, 0, 2), loads):
        copy.wait()
        for r in range(3 * i, 3 * i + 3):
            mb[r] = mf[r].astype(BF16)

    pl.semaphore_wait(barrier, 4)

    def start_direct(src, buf, send, recv):
        out = {}
        k = 0
        for r in (4, 7, 1):
            for ay in (1, -1):
                out[(r, ay)] = remote(
                    src.at[pl.ds(r, 1)], buf.at[pl.ds(9 * code(0, -ay) + r, 1)],
                    send.at[k], recv.at[k], (0, ay),
                )
                k += 1
        for name, d in (("off", off), ("on", on)):
            for i, r in enumerate((4, 3, 5, rows_of(d), rows_of(d) + 2)):
                out[(name, i)] = remote(
                    src.at[pl.ds(r, 1)], buf.at[pl.ds(9 * code(-d, 0) + r, 1)],
                    send.at[k], recv.at[k], (d, 0),
                )
                k += 1
        for copy in out.values():
            copy.start()
        return out

    def start_relays(sent, buf, diag, send, recv):
        near, odd, extra = [], [], []
        for j, w in enumerate((1, -1)):
            near.append(remote(
                buf.at[pl.ds(9 * code(0, w) + 4, 1)], diag.at[pl.ds(code(-on, w), 1)],
                send.at[16 + j], recv.at[16 + j], (on, 0),
            ))
            odd.append(remote(
                buf.at[pl.ds(9 * code(0, w) + 4, 1)], diag.at[pl.ds(code(-off, w), 1)],
                send.at[18 + j], recv.at[18 + j], (off, 0),
            ))
            extra.append(remote(
                buf.at[pl.ds(9 * code(off, 0) + 4, 1)], diag.at[pl.ds(code(off, w), 1)],
                send.at[20 + j], recv.at[18 + j], (0, -w),
            ))
        sent[("off", 0)].wait_recv()
        for copy in extra:
            pl.when(core == 1)(copy.start)
        sent[(4, 1)].wait_recv()
        sent[(4, -1)].wait_recv()
        for copy in odd:
            pl.when(core == 1)(copy.start)
        for copy in near:
            copy.start()
        return near, odd, extra

    def wait_direct(sent):
        for key, copy in sent.items():
            if key not in ((4, 1), (4, -1), ("off", 0)):
                copy.wait_recv()

    def wait_relayed(relays):
        for copy in relays[0] + relays[1]:
            copy.wait_recv()

    def wait_sent(sent, relays):
        for copy in list(sent.values()) + relays[0]:
            copy.wait_send()
        for copy in relays[1] + relays[2]:
            pl.when(core == 1)(copy.wait_send)

    msent = start_direct(mb, mbuf, msend, mrecv)

    listed.wait()
    cd = [codes[0, 0, p] for p in range(SLOTS)]
    live = [p < counts[0, 0] for p in range(SLOTS)]
    ox = [c // 3 - 1 for c in cd]
    oy = [c % 3 - 1 for c in cd]

    def pair(p, q):
        rx, ry = ox[p] - ox[q], oy[p] - oy[q]
        ok = (jnp.abs(rx) <= 1) & (jnp.abs(ry) <= 1) & live[p] & live[q]
        return ok, (rx + 1) * 3 + ry + 1

    rank = [jnp.where(ox[p] == 0, 1, jnp.where(oy[p] == 0, 2, 0)) for p in range(SLOTS)]

    def centre(dst, mine):
        for p in range(SLOTS):
            block = mine[jnp.where(live[p], cd[p], 9)]
            dst[sl(p), sl(0)] = block
            if p:
                dst[sl(0), sl(p)] = block.T

    def others(dst, buf, diag):
        for p in range(1, SLOTS):
            edge = rank[p] > 0
            block = buf[jnp.where(live[p] & edge, cd[p] * 9 + 4, 81)]
            far = diag[jnp.where(live[p] & jnp.logical_not(edge), cd[p], 9)]
            dst[sl(p), sl(p)] = block + far
        for p in range(1, SLOTS):
            for q in range(p + 1, SLOTS):
                ok, r = pair(p, q)
                swap = rank[p] > rank[q]
                spot = jnp.where(swap, cd[p] * 9 + 8 - r, cd[q] * 9 + r)
                block = buf[jnp.where(ok, spot, 81)].astype(F32)
                turned = block.T
                flag = jnp.where(swap, 1.0, 0.0).astype(F32)
                keep = 1.0 - flag
                dst[sl(p), sl(q)] = (keep * block + flag * turned).astype(BF16)
                dst[sl(q), sl(p)] = (keep * turned + flag * block).astype(BF16)

    centre(es, mb)
    mrelay = start_relays(msent, mbuf, mdiag, msend, mrecv)
    hsent = start_direct(ham.at[0, 0], hbuf, hsend, hrecv)
    wait_direct(msent)
    wait_relayed(mrelay)
    others(es, mbuf, mdiag)

    row = lax.broadcasted_iota(jnp.int32, (N, B), 0)
    col = lax.broadcasted_iota(jnp.int32, (N, B), 1)
    first = jnp.where(row == col, 1.0, 0.0).astype(F32) - es[:, :B].astype(F32)
    e2[:, :N] = dot(es[...], es[...]).astype(BF16)
    e2[:, N:] = first.astype(BF16)
    both = dot(e2[:, :N], e2[...])
    e4[...] = both[:, :N].astype(BF16)
    total = first + both[:, N:]
    term = total.astype(BF16)
    for step in range(3):
        image = dot(e4[...], term)
        total = total + image
        term = image.astype(BF16)
    for p in range(SLOTS):
        xs[p] = total[sl(p), :]

    for c in range(9):
        spot = jnp.int32(SLOTS)
        for p in range(SLOTS):
            spot = jnp.where(live[p] & (cd[p] == c), p, spot)
        wire[c] = xs[spot].astype(BF16)

    zsent, xsent, relayed = {}, [], []
    rows = ((0, 0), (0, 1), (off, 0), (off, 1), (on, 0), (on, 1))
    k = 0
    for i, (rx, half) in enumerate(rows):
        for ay in (1, -1):
            r = rows_of(rx) + half + (1 if ay == 1 else 0)
            copy = remote(
                wire.at[pl.ds(r, 1)], ibuf.at[pl.ds(9 * code(0, -ay) + r, 1)],
                isend.at[k], irecv.at[k], (0, ay),
            )
            copy.start()
            zsent[(i, ay)] = copy
            k += 1
    for d in (off, on):
        first = 3 * ((d + 1) // 2)
        copy = remote(
            wire.at[pl.ds(first, 6)], ibuf.at[pl.ds(9 * code(-d, 0) + first, 6)],
            isend.at[k], irecv.at[k], (d, 0),
        )
        copy.start()
        xsent.append(copy)
        k += 1

    def relay(i, w, d, k):
        rx, half = rows[i]
        r = rows_of(rx) + half + (1 if w == -1 else 0)
        copy = remote(
            ibuf.at[pl.ds(9 * code(0, w) + r, 1)],
            ibuf.at[pl.ds(9 * code(-d, w) + r, 1)],
            isend.at[k], irecv.at[k], (d, 0),
        )
        copy.start()
        relayed.append(copy)

    hrelay = start_relays(hsent, hbuf, hdiag, hsend, hrecv)
    own.wait()
    centre(hs, hown)
    for i in range(4):
        for w in (1, -1):
            zsent[(i, -w)].wait_recv()
            relay(i, w, off, k)
            k += 1
    for i in (0, 1):
        for w in (1, -1):
            relay(i, w, on, k)
            k += 1
    for i in (4, 5):
        for w in (1, -1):
            zsent[(i, -w)].wait_recv()
            relay(i, w, on, k)
            k += 1

    wait_direct(hsent)
    wait_relayed(hrelay)
    others(hs, hbuf, hdiag)
    for p in range(SLOTS):
        isub[sl(p), sl(0)] = wire[jnp.where(live[p], cd[p], 9)]
    for copy in xsent + relayed:
        copy.wait_recv()
    for q in range(1, SLOTS):
        for p in range(SLOTS):
            ok, r = pair(p, q)
            isub[sl(p), sl(q)] = ibuf[jnp.where(ok, cd[q] * 9 + r, 81)]

    wait_sent(msent, mrelay)
    wait_sent(hsent, hrelay)
    for copy in list(zsent.values()) + xsent + relayed:
        copy.wait_send()


def sign_kernel(
    codes_hbm, counts, isub, hs, xs, inv_out, den_out,
    codes, s, h, g, q, ds, sem,
):
    listed = pltpu.make_async_copy(codes_hbm, codes, sem.at[18])
    listed.start()
    ds[SLOTS] = jnp.zeros((B, B), F32)

    product = dot(isub[...], hs[...])
    s[...] = product
    h[...] = product.astype(BF16)
    norm = jnp.sum(jnp.sum(product * product, axis=0, keepdims=True), keepdims=True) / N
    scale = 1.0 / (3.0 * jnp.sqrt(norm) + 1e-6)

    listed.wait()
    count = counts[0, 0]
    spots = []
    for c in range(9):
        at = jnp.int32(SLOTS)
        for p in range(SLOTS):
            at = jnp.where((p < count) & (codes[0, 0, p] == c), p, at)
        spots.append(at)
    inv, blank = [], []
    for c in range(9):
        inv.append(pltpu.make_async_copy(xs.at[spots[c]], inv_out.at[0, 0, c], sem.at[c]))
        blank.append(pltpu.make_async_copy(ds.at[SLOTS], den_out.at[0, 0, c], sem.at[9 + c]))
    for c in range(9):
        inv[c].start()
        pl.when(spots[c] == SLOTS)(blank[c].start)

    a, b = h, g
    for step in range(SIGN - 1):
        square = dot(a[...], a[...])
        q[...] = (square * (scale * scale) if step == 0 else square).astype(BF16)
        new = 1.5 * s[...] - 0.5 * dot(a[...], q[...])
        if step == 0:
            new = new * scale
        s[...] = new
        b[...] = new.astype(BF16)
        a, b = b, a
    q[:, :B] = dot(a[...], a[:, :B]).astype(BF16)
    rows = lax.broadcasted_iota(jnp.int32, (B, B), 0)
    cols = lax.broadcasted_iota(jnp.int32, (B, B), 1)
    ident = jnp.where(rows == cols, 0.5, 0.0).astype(F32)
    for p in range(SLOTS):
        last = 1.5 * s[sl(p), :B] - 0.5 * dot(a[sl(p), :], q[:, :B])
        ds[p] = ident - 0.5 * last if p == 0 else -0.5 * last
        c = codes[0, 0, p]
        copy = pltpu.make_async_copy(ds.at[p], den_out.at[0, 0, c], sem.at[9 + c])
        pl.when(p < count)(copy.start)
    for copy in inv + blank:
        copy.wait()


def local(margin_dev, hamiltonian, slot_codes, slot_count):
    vm = pl.BlockSpec(memory_space=pltpu.VMEM)
    hbm = pl.BlockSpec(memory_space=pltpu.HBM)
    shape = jax.ShapeDtypeStruct
    dma = pltpu.SemaphoreType.DMA
    n_sym = 22
    sm = pl.BlockSpec(memory_space=pltpu.SMEM)
    slot_codes, margin_dev, hamiltonian = (
        pltpu.with_memory_space_constraint(x, pltpu.HBM)
        for x in (slot_codes, margin_dev, hamiltonian)
    )
    xs, hs, isub = pl.pallas_call(
        exchange_kernel,
        out_shape=(
            shape((SLOTS + 1, B, B), F32),
            shape((N, N), BF16),
            shape((N, N), BF16),
        ),
        in_specs=[hbm, sm, hbm, hbm],
        out_specs=(vm, vm, vm),
        scratch_shapes=[
            pltpu.SMEM((1, 1, SLOTS), jnp.int32),
            pltpu.VMEM((9, B, B), F32),
            pltpu.VMEM((10, B, B), BF16),
            pltpu.VMEM((82, B, B), BF16),
            pltpu.VMEM((10, B, B), BF16),
            pltpu.VMEM((10, B, B), BF16),
            pltpu.VMEM((82, B, B), BF16),
            pltpu.VMEM((10, B, B), BF16),
            pltpu.VMEM((82, B, B), BF16),
            pltpu.VMEM((10, B, B), BF16),
            pltpu.VMEM((N, N), BF16),
            pltpu.VMEM((N, N + B), BF16),
            pltpu.VMEM((N, N), BF16),
            dma((5,)),
            dma((n_sym,)),
            dma((n_sym,)),
            dma((n_sym,)),
            dma((n_sym,)),
            dma((30,)),
            dma((30,)),
        ],
        compiler_params=pltpu.CompilerParams(
            collective_id=0, has_side_effects=True, vmem_limit_bytes=32 << 20
        ),
        name="exchange",
    )(slot_codes, slot_count, margin_dev, hamiltonian)
    return pl.pallas_call(
        sign_kernel,
        out_shape=(
            shape((1, 1, 9, B, B), F32),
            shape((1, 1, 9, B, B), F32),
        ),
        in_specs=[hbm, sm, vm, vm, vm],
        out_specs=(hbm, hbm),
        scratch_shapes=[
            pltpu.SMEM((1, 1, SLOTS), jnp.int32),
            pltpu.VMEM((N, N), F32),
            pltpu.VMEM((N, N), BF16),
            pltpu.VMEM((N, N), BF16),
            pltpu.VMEM((N, N), BF16),
            pltpu.VMEM((SLOTS + 1, B, B), F32),
            dma((19,)),
        ],
        compiler_params=pltpu.CompilerParams(vmem_limit_bytes=32 << 20),
        name="sign",
    )(slot_codes, slot_count, isub, hs, xs)


def solution(mesh):
    return jax.shard_map(
        local,
        mesh=mesh,
        in_specs=(
            P("gx", "gy", None, None, None),
            P("gx", "gy", None, None, None),
            P("gx", "gy", None),
            P("gx", "gy"),
        ),
        out_specs=(P("gx", "gy", None, None, None), P("gx", "gy", None, None, None)),
        check_vma=False,
    )
```

```python
import jax
import jax.numpy as jnp
from jax import lax
from jax.experimental import pallas as pl
from jax.experimental.pallas import tpu as pltpu
from jax.sharding import PartitionSpec as P

B = 128
SLOTS = 5
N = SLOTS * B
SIGN = 4
MESH = pl.DeviceIdType.MESH
F32 = jnp.float32
BF16 = jnp.bfloat16
EDGES = ((0, 1), (0, -1), (1, 0), (-1, 0))


def code(dx, dy):
    return 3 * (dx + 1) + dy + 1


def dot(a, b):
    return jnp.dot(a, b, preferred_element_type=F32)


def sl(p):
    return slice(p * B, (p + 1) * B)


def rows_of(step):
    return 3 * (step + 1)


def exchange_kernel(
    codes_hbm, counts, margin, ham,
    xs, hs, isub,
    codes, mf, mb, mbuf, mdiag, hown, hbuf, hdiag, ibuf, wire, es, e2, e4,
    lsem, msend, mrecv, hsend, hrecv, isend, irecv,
):
    nu, nv = lax.axis_size("gx"), lax.axis_size("gy")
    u, v = lax.axis_index("gx"), lax.axis_index("gy")
    core = lax.rem(u, 2)
    off = 2 * core - 1
    on = -off

    def dev(a):
        return (lax.rem(u + a[0] + nu, nu), lax.rem(v + a[1] + nv, nv))

    def remote(src, dst, send, recv, a):
        return pltpu.make_async_remote_copy(
            src_ref=src, dst_ref=dst, send_sem=send, recv_sem=recv,
            device_id=dev(a), device_id_type=MESH,
        )

    barrier = pltpu.get_barrier_semaphore()
    for a in EDGES:
        pl.semaphore_signal(barrier, inc=1, device_id=dev(a), device_id_type=MESH)

    loads = [
        pltpu.make_async_copy(
            margin.at[0, 0, pl.ds(3 * i, 3)], mf.at[pl.ds(3 * i, 3)], lsem.at[i]
        )
        for i in (1, 0, 2)
    ]
    listed = pltpu.make_async_copy(codes_hbm, codes, lsem.at[4])
    own = pltpu.make_async_copy(ham.at[0, 0], hown.at[pl.ds(0, 9)], lsem.at[3])
    for copy in loads + [listed, own]:
        copy.start()

    zero = jnp.zeros((B, B), BF16)
    mb[9] = zero
    hown[9] = zero
    wire[9] = zero
    mbuf[81] = zero
    hbuf[81] = zero
    mdiag[9] = zero
    hdiag[9] = zero
    ibuf[81] = zero
    xs[SLOTS] = jnp.zeros((B, B), F32)

    for i, copy in zip((1, 0, 2), loads):
        copy.wait()
        for r in range(3 * i, 3 * i + 3):
            mb[r] = mf[r].astype(BF16)

    pl.semaphore_wait(barrier, 4)

    def start_direct(src, buf, send, recv):
        out = {}
        k = 0
        for r in (4, 7, 1):
            for ay in (1, -1):
                out[(r, ay)] = remote(
                    src.at[pl.ds(r, 1)], buf.at[pl.ds(9 * code(0, -ay) + r, 1)],
                    send.at[k], recv.at[k], (0, ay),
                )
                k += 1
        for name, d in (("off", off), ("on", on)):
            for i, r in enumerate((4, 3, 5, rows_of(d), rows_of(d) + 2)):
                out[(name, i)] = remote(
                    src.at[pl.ds(r, 1)], buf.at[pl.ds(9 * code(-d, 0) + r, 1)],
                    send.at[k], recv.at[k], (d, 0),
                )
                k += 1
        for copy in out.values():
            copy.start()
        return out

    def start_relays(sent, buf, diag, send, recv):
        near, odd, extra = [], [], []
        for j, w in enumerate((1, -1)):
            near.append(remote(
                buf.at[pl.ds(9 * code(0, w) + 4, 1)], diag.at[pl.ds(code(-on, w), 1)],
                send.at[16 + j], recv.at[16 + j], (on, 0),
            ))
            odd.append(remote(
                buf.at[pl.ds(9 * code(0, w) + 4, 1)], diag.at[pl.ds(code(-off, w), 1)],
                send.at[18 + j], recv.at[18 + j], (off, 0),
            ))
            extra.append(remote(
                buf.at[pl.ds(9 * code(off, 0) + 4, 1)], diag.at[pl.ds(code(off, w), 1)],
                send.at[20 + j], recv.at[18 + j], (0, -w),
            ))
        sent[("off", 0)].wait_recv()
        for copy in extra:
            pl.when(core == 1)(copy.start)
        sent[(4, 1)].wait_recv()
        sent[(4, -1)].wait_recv()
        for copy in odd:
            pl.when(core == 1)(copy.start)
        for copy in near:
            copy.start()
        return near, odd, extra

    def wait_direct(sent):
        for key, copy in sent.items():
            if key not in ((4, 1), (4, -1), ("off", 0)):
                copy.wait_recv()

    def wait_relayed(relays):
        for copy in relays[0] + relays[1]:
            copy.wait_recv()

    def wait_sent(sent, relays):
        for copy in list(sent.values()) + relays[0]:
            copy.wait_send()
        for copy in relays[1] + relays[2]:
            pl.when(core == 1)(copy.wait_send)

    msent = start_direct(mb, mbuf, msend, mrecv)

    listed.wait()
    cd = [codes[0, 0, p] for p in range(SLOTS)]
    live = [p < counts[0, 0] for p in range(SLOTS)]
    ox = [c // 3 - 1 for c in cd]
    oy = [c % 3 - 1 for c in cd]

    def pair(p, q):
        rx, ry = ox[p] - ox[q], oy[p] - oy[q]
        ok = (jnp.abs(rx) <= 1) & (jnp.abs(ry) <= 1) & live[p] & live[q]
        return ok, (rx + 1) * 3 + ry + 1

    rank = [jnp.where(ox[p] == 0, 1, jnp.where(oy[p] == 0, 2, 0)) for p in range(SLOTS)]

    def centre(dst, mine):
        for p in range(SLOTS):
            block = mine[jnp.where(live[p], cd[p], 9)]
            dst[sl(p), sl(0)] = block
            if p:
                dst[sl(0), sl(p)] = block.T

    def others(dst, buf, diag):
        for p in range(1, SLOTS):
            edge = rank[p] > 0
            block = buf[jnp.where(live[p] & edge, cd[p] * 9 + 4, 81)]
            far = diag[jnp.where(live[p] & jnp.logical_not(edge), cd[p], 9)]
            dst[sl(p), sl(p)] = block + far
        for p in range(1, SLOTS):
            for q in range(p + 1, SLOTS):
                ok, r = pair(p, q)
                swap = rank[p] > rank[q]
                spot = jnp.where(swap, cd[p] * 9 + 8 - r, cd[q] * 9 + r)
                block = buf[jnp.where(ok, spot, 81)].astype(F32)
                turned = block.T
                flag = jnp.where(swap, 1.0, 0.0).astype(F32)
                keep = 1.0 - flag
                dst[sl(p), sl(q)] = (keep * block + flag * turned).astype(BF16)
                dst[sl(q), sl(p)] = (keep * turned + flag * block).astype(BF16)

    centre(es, mb)
    mrelay = start_relays(msent, mbuf, mdiag, msend, mrecv)
    hsent = start_direct(ham.at[0, 0], hbuf, hsend, hrecv)
    wait_direct(msent)
    wait_relayed(mrelay)
    others(es, mbuf, mdiag)

    row = lax.broadcasted_iota(jnp.int32, (N, B), 0)
    col = lax.broadcasted_iota(jnp.int32, (N, B), 1)
    first = jnp.where(row == col, 1.0, 0.0).astype(F32) - es[:, :B].astype(F32)
    e2[:, :N] = dot(es[...], es[...]).astype(BF16)
    e2[:, N:] = first.astype(BF16)
    both = dot(e2[:, :N], e2[...])
    e4[...] = both[:, :N].astype(BF16)
    total = first + both[:, N:]
    term = total.astype(BF16)
    for step in range(3):
        image = dot(e4[...], term)
        total = total + image
        term = image.astype(BF16)
    for p in range(SLOTS):
        xs[p] = total[sl(p), :]

    for c in range(9):
        spot = jnp.int32(SLOTS)
        for p in range(SLOTS):
            spot = jnp.where(live[p] & (cd[p] == c), p, spot)
        wire[c] = xs[spot].astype(BF16)

    zsent, xsent = {}, []
    rows = {"mid": 0, "off": off, "on": on}
    k = 0
    for name, rx in rows.items():
        for far in (1, 0):
            for ay in (1, -1):
                r = rows_of(rx) + 1 + far * ay
                zsent[(name, far, ay)] = remote(
                    wire.at[pl.ds(r, 1)], ibuf.at[pl.ds(9 * code(0, -ay) + r, 1)],
                    isend.at[k], irecv.at[k], (0, ay),
                )
                k += 1

    def start_along(order):
        for name, far in order:
            for ay in (1, -1):
                zsent[(name, far, ay)].start()

    pl.when(core == 0)(lambda: start_along((
        ("mid", 1), ("off", 1), ("mid", 0), ("on", 1), ("on", 0), ("off", 0)
    )))
    pl.when(core == 1)(lambda: start_along((
        ("mid", 1), ("off", 1), ("mid", 0), ("off", 0), ("on", 1), ("on", 0)
    )))
    for d, r, n in (
        (off, 4, 1), (off, rows_of(off) + 1, 1), (off, 3, 1), (off, 5, 1),
        (off, rows_of(off), 1), (off, rows_of(off) + 2, 1), (on, 3 * ((on + 1) // 2), 6),
    ):
        copy = remote(
            wire.at[pl.ds(r, n)], ibuf.at[pl.ds(9 * code(-d, 0) + r, n)],
            isend.at[k], irecv.at[k], (d, 0),
        )
        copy.start()
        xsent.append(copy)
        k += 1

    def relay(o, t, r, a, send, recv):
        return remote(
            ibuf.at[pl.ds(9 * code(*o) + r, 1)], ibuf.at[pl.ds(9 * code(*t) + r, 1)],
            isend.at[send], irecv.at[recv], a,
        )

    along_u, along_v, inside = {}, [], {}
    for name in ("mid", "off"):
        for far in (1, 0):
            for w in (1, -1):
                r = rows_of(rows[name]) + 1 - far * w
                along_u[(name, far, w)] = relay((0, w), (-off, w), r, (off, 0), k, k)
                if far == 0:
                    r = 4 if name == "mid" else rows_of(-off) + 1
                    along_v.append(relay((off, 0), (off, w), r, (0, -w), k + 16, k))
                k += 1
    for name in ("mid", "on"):
        for far in (1, 0):
            for w in (1, -1):
                r = rows_of(rows[name]) + 1 - far * w
                inside[(name, far, w)] = relay((0, w), (-on, w), r, (on, 0), k, k)
                k += 1

    def arrived(name, far, then=()):
        for w in (1, -1):
            zsent[(name, far, -w)].wait_recv()
            for copies in then:
                copies[(name, far, w)].start()

    def pass_on(name, far):
        for w in (1, -1):
            inside[(name, far, w)].start()

    def even_relays():
        arrived("mid", 1, (along_u,))
        arrived("off", 1, (along_u,))
        pass_on("mid", 1)
        arrived("mid", 0, (inside,))
        arrived("on", 1, (inside,))
        arrived("on", 0, (inside,))
        arrived("off", 0)
        for copy in xsent[:2]:
            copy.wait_recv()

    def odd_relays():
        arrived("mid", 1, (along_u,))
        for copy in xsent[:2]:
            copy.wait_recv()
        for copy in along_v:
            copy.start()
        arrived("off", 1, (along_u,))
        arrived("mid", 0, (along_u,))
        arrived("off", 0, (along_u,))
        pass_on("mid", 1)
        pass_on("mid", 0)
        arrived("on", 1, (inside,))
        arrived("on", 0, (inside,))

    hrelay = start_relays(hsent, hbuf, hdiag, hsend, hrecv)
    own.wait()
    centre(hs, hown)
    pl.when(core == 0)(even_relays)
    pl.when(core == 1)(odd_relays)

    wait_direct(hsent)
    wait_relayed(hrelay)
    others(hs, hbuf, hdiag)
    for p in range(SLOTS):
        isub[sl(p), sl(0)] = wire[jnp.where(live[p], cd[p], 9)]
    for copy in xsent[2:] + list(along_u.values()) + list(inside.values()):
        copy.wait_recv()
    for q in range(1, SLOTS):
        for p in range(SLOTS):
            ok, r = pair(p, q)
            isub[sl(p), sl(q)] = ibuf[jnp.where(ok, cd[q] * 9 + r, 81)]

    wait_sent(msent, mrelay)
    wait_sent(hsent, hrelay)
    for copy in list(zsent.values()) + xsent + list(inside.values()):
        copy.wait_send()
    for (name, far, w), copy in along_u.items():
        if far == 1:
            copy.wait_send()
        else:
            pl.when(core == 1)(copy.wait_send)
    for copy in along_v:
        pl.when(core == 1)(copy.wait_send)


def sign_kernel(
    codes_hbm, counts, isub, hs, xs, inv_out, den_out,
    codes, s, h, g, q, ds, sem,
):
    listed = pltpu.make_async_copy(codes_hbm, codes, sem.at[18])
    listed.start()
    ds[SLOTS] = jnp.zeros((B, B), F32)

    product = dot(isub[...], hs[...])
    s[...] = product
    h[...] = product.astype(BF16)
    norm = jnp.sum(jnp.sum(product * product, axis=0, keepdims=True), keepdims=True) / N
    scale = 1.0 / (3.0 * jnp.sqrt(norm) + 1e-6)

    listed.wait()
    count = counts[0, 0]
    spots = []
    for c in range(9):
        at = jnp.int32(SLOTS)
        for p in range(SLOTS):
            at = jnp.where((p < count) & (codes[0, 0, p] == c), p, at)
        spots.append(at)
    inv, blank = [], []
    for c in range(9):
        inv.append(pltpu.make_async_copy(xs.at[spots[c]], inv_out.at[0, 0, c], sem.at[c]))
        blank.append(pltpu.make_async_copy(ds.at[SLOTS], den_out.at[0, 0, c], sem.at[9 + c]))
    for c in range(9):
        inv[c].start()
        pl.when(spots[c] == SLOTS)(blank[c].start)

    a, b = h, g
    for step in range(SIGN - 1):
        square = dot(a[...], a[...])
        q[...] = (square * (scale * scale) if step == 0 else square).astype(BF16)
        new = 1.5 * s[...] - 0.5 * dot(a[...], q[...])
        if step == 0:
            new = new * scale
        s[...] = new
        b[...] = new.astype(BF16)
        a, b = b, a
    q[:, :B] = dot(a[...], a[:, :B]).astype(BF16)
    rows = lax.broadcasted_iota(jnp.int32, (B, B), 0)
    cols = lax.broadcasted_iota(jnp.int32, (B, B), 1)
    ident = jnp.where(rows == cols, 0.5, 0.0).astype(F32)
    for p in range(SLOTS):
        last = 1.5 * s[sl(p), :B] - 0.5 * dot(a[sl(p), :], q[:, :B])
        ds[p] = ident - 0.5 * last if p == 0 else -0.5 * last
        c = codes[0, 0, p]
        copy = pltpu.make_async_copy(ds.at[p], den_out.at[0, 0, c], sem.at[9 + c])
        pl.when(p < count)(copy.start)
    for copy in inv + blank:
        copy.wait()


def local(margin_dev, hamiltonian, slot_codes, slot_count):
    vm = pl.BlockSpec(memory_space=pltpu.VMEM)
    hbm = pl.BlockSpec(memory_space=pltpu.HBM)
    shape = jax.ShapeDtypeStruct
    dma = pltpu.SemaphoreType.DMA
    n_sym = 22
    sm = pl.BlockSpec(memory_space=pltpu.SMEM)
    slot_codes, margin_dev, hamiltonian = (
        pltpu.with_memory_space_constraint(x, pltpu.HBM)
        for x in (slot_codes, margin_dev, hamiltonian)
    )
    xs, hs, isub = pl.pallas_call(
        exchange_kernel,
        out_shape=(
            shape((SLOTS + 1, B, B), F32),
            shape((N, N), BF16),
            shape((N, N), BF16),
        ),
        in_specs=[hbm, sm, hbm, hbm],
        out_specs=(vm, vm, vm),
        scratch_shapes=[
            pltpu.SMEM((1, 1, SLOTS), jnp.int32),
            pltpu.VMEM((9, B, B), F32),
            pltpu.VMEM((10, B, B), BF16),
            pltpu.VMEM((82, B, B), BF16),
            pltpu.VMEM((10, B, B), BF16),
            pltpu.VMEM((10, B, B), BF16),
            pltpu.VMEM((82, B, B), BF16),
            pltpu.VMEM((10, B, B), BF16),
            pltpu.VMEM((82, B, B), BF16),
            pltpu.VMEM((10, B, B), BF16),
            pltpu.VMEM((N, N), BF16),
            pltpu.VMEM((N, N + B), BF16),
            pltpu.VMEM((N, N), BF16),
            dma((5,)),
            dma((n_sym,)),
            dma((n_sym,)),
            dma((n_sym,)),
            dma((n_sym,)),
            dma((43,)),
            dma((35,)),
        ],
        compiler_params=pltpu.CompilerParams(
            collective_id=0, has_side_effects=True, vmem_limit_bytes=32 << 20
        ),
        name="exchange",
    )(slot_codes, slot_count, margin_dev, hamiltonian)
    return pl.pallas_call(
        sign_kernel,
        out_shape=(
            shape((1, 1, 9, B, B), F32),
            shape((1, 1, 9, B, B), F32),
        ),
        in_specs=[hbm, sm, vm, vm, vm],
        out_specs=(hbm, hbm),
        scratch_shapes=[
            pltpu.SMEM((1, 1, SLOTS), jnp.int32),
            pltpu.VMEM((N, N), F32),
            pltpu.VMEM((N, N), BF16),
            pltpu.VMEM((N, N), BF16),
            pltpu.VMEM((N, N), BF16),
            pltpu.VMEM((SLOTS + 1, B, B), F32),
            dma((19,)),
        ],
        compiler_params=pltpu.CompilerParams(vmem_limit_bytes=32 << 20),
        name="sign",
    )(slot_codes, slot_count, isub, hs, xs)


def solution(mesh):
    return jax.shard_map(
        local,
        mesh=mesh,
        in_specs=(
            P("gx", "gy", None, None, None),
            P("gx", "gy", None, None, None),
            P("gx", "gy", None),
            P("gx", "gy"),
        ),
        out_specs=(P("gx", "gy", None, None, None), P("gx", "gy", None, None, None)),
        check_vma=False,
    )
```

```python
import functools

import jax
import jax.numpy as jnp
from jax import lax
from jax.experimental import pallas as pl
from jax.experimental.pallas import tpu as pltpu
from jax.sharding import PartitionSpec as P

B = 128
SLOTS = 5
N = SLOTS * B
SIGN = 4
MESH = pl.DeviceIdType.MESH
F32 = jnp.float32
BF16 = jnp.bfloat16
EDGES = ((0, 1), (0, -1), (1, 0), (-1, 0))


def code(dx, dy):
    return 3 * (dx + 1) + dy + 1


def dot(a, b):
    return jnp.dot(a, b, preferred_element_type=F32)


def sl(p):
    return slice(p * B, (p + 1) * B)


def rows_of(step):
    return 3 * (step + 1)


def exchange_kernel(
    codes_hbm, counts, margin, ham,
    xs, hs, isub,
    codes, mf, mb, mbuf, mdiag, hown, hbuf, hdiag, ibuf, wire, es, e2, e4,
    lsem, msend, mrecv, hsend, hrecv, isend, irecv,
):
    nu, nv = lax.axis_size("gx"), lax.axis_size("gy")
    u, v = lax.axis_index("gx"), lax.axis_index("gy")
    core = lax.rem(u, 2)
    off = 2 * core - 1
    on = -off

    def dev(a):
        return (lax.rem(u + a[0] + nu, nu), lax.rem(v + a[1] + nv, nv))

    def remote(src, dst, send, recv, a):
        return pltpu.make_async_remote_copy(
            src_ref=src, dst_ref=dst, send_sem=send, recv_sem=recv,
            device_id=dev(a), device_id_type=MESH,
        )

    barrier = pltpu.get_barrier_semaphore()
    for a in EDGES:
        pl.semaphore_signal(barrier, inc=1, device_id=dev(a), device_id_type=MESH)

    loads = [
        pltpu.make_async_copy(
            margin.at[0, 0, pl.ds(3 * i, 3)], mf.at[pl.ds(3 * i, 3)], lsem.at[i]
        )
        for i in (1, 0, 2)
    ]
    listed = pltpu.make_async_copy(codes_hbm, codes, lsem.at[4])
    own = pltpu.make_async_copy(ham.at[0, 0], hown.at[pl.ds(0, 9)], lsem.at[3])
    for copy in loads + [listed, own]:
        copy.start()

    zero = jnp.zeros((B, B), BF16)
    mb[9] = zero
    hown[9] = zero
    wire[9] = zero
    mbuf[81] = zero
    hbuf[81] = zero
    mdiag[9] = zero
    hdiag[9] = zero
    ibuf[81] = zero
    xs[SLOTS] = jnp.zeros((B, B), F32)

    for i, copy in zip((1, 0, 2), loads):
        copy.wait()
        for r in range(3 * i, 3 * i + 3):
            mb[r] = mf[r].astype(BF16)

    pl.semaphore_wait(barrier, 4)

    def start_direct(src, buf, send, recv):
        out = {}
        k = 0
        for r in (4, 7, 1):
            for ay in (1, -1):
                out[(r, ay)] = remote(
                    src.at[pl.ds(r, 1)], buf.at[pl.ds(9 * code(0, -ay) + r, 1)],
                    send.at[k], recv.at[k], (0, ay),
                )
                k += 1
        for name, d in (("off", off), ("on", on)):
            for i, r in enumerate((4, 3, 5, rows_of(d), rows_of(d) + 2)):
                out[(name, i)] = remote(
                    src.at[pl.ds(r, 1)], buf.at[pl.ds(9 * code(-d, 0) + r, 1)],
                    send.at[k], recv.at[k], (d, 0),
                )
                k += 1
        for copy in out.values():
            copy.start()
        return out

    def start_relays(sent, buf, diag, send, recv):
        near, odd, extra = [], [], []
        for j, w in enumerate((1, -1)):
            near.append(remote(
                buf.at[pl.ds(9 * code(0, w) + 4, 1)], diag.at[pl.ds(code(-on, w), 1)],
                send.at[16 + j], recv.at[16 + j], (on, 0),
            ))
            odd.append(remote(
                buf.at[pl.ds(9 * code(0, w) + 4, 1)], diag.at[pl.ds(code(-off, w), 1)],
                send.at[18 + j], recv.at[18 + j], (off, 0),
            ))
            extra.append(remote(
                buf.at[pl.ds(9 * code(off, 0) + 4, 1)], diag.at[pl.ds(code(off, w), 1)],
                send.at[20 + j], recv.at[18 + j], (0, -w),
            ))
        sent[("off", 0)].wait_recv()
        for copy in extra:
            pl.when(core == 1)(copy.start)
        sent[(4, 1)].wait_recv()
        sent[(4, -1)].wait_recv()
        for copy in odd:
            pl.when(core == 1)(copy.start)
        for copy in near:
            copy.start()
        return near, odd, extra

    def wait_direct(sent):
        for key, copy in sent.items():
            if key not in ((4, 1), (4, -1), ("off", 0)):
                copy.wait_recv()

    def wait_relayed(relays):
        for copy in relays[0] + relays[1]:
            copy.wait_recv()

    def wait_sent(sent, relays):
        for copy in list(sent.values()) + relays[0]:
            copy.wait_send()
        for copy in relays[1] + relays[2]:
            pl.when(core == 1)(copy.wait_send)

    msent = start_direct(mb, mbuf, msend, mrecv)

    listed.wait()
    cd = [codes[0, 0, p] for p in range(SLOTS)]
    live = [p < counts[0, 0] for p in range(SLOTS)]
    ox = [c // 3 - 1 for c in cd]
    oy = [c % 3 - 1 for c in cd]

    def pair(p, q):
        rx, ry = ox[p] - ox[q], oy[p] - oy[q]
        ok = (jnp.abs(rx) <= 1) & (jnp.abs(ry) <= 1) & live[p] & live[q]
        return ok, (rx + 1) * 3 + ry + 1

    rank = [jnp.where(ox[p] == 0, 1, jnp.where(oy[p] == 0, 2, 0)) for p in range(SLOTS)]

    def centre(dst, mine):
        for p in range(SLOTS):
            block = mine[jnp.where(live[p], cd[p], 9)]
            dst[sl(p), sl(0)] = block
            if p:
                dst[sl(0), sl(p)] = block.T

    def others(dst, buf, diag):
        for p in range(1, SLOTS):
            edge = rank[p] > 0
            block = buf[jnp.where(live[p] & edge, cd[p] * 9 + 4, 81)]
            far = diag[jnp.where(live[p] & jnp.logical_not(edge), cd[p], 9)]
            dst[sl(p), sl(p)] = block + far
        for p in range(1, SLOTS):
            for q in range(p + 1, SLOTS):
                ok, r = pair(p, q)
                swap = rank[p] > rank[q]
                spot = jnp.where(swap, cd[p] * 9 + 8 - r, cd[q] * 9 + r)
                block = buf[jnp.where(ok, spot, 81)].astype(F32)
                turned = block.T
                flag = jnp.where(swap, 1.0, 0.0).astype(F32)
                keep = 1.0 - flag
                dst[sl(p), sl(q)] = (keep * block + flag * turned).astype(BF16)
                dst[sl(q), sl(p)] = (keep * turned + flag * block).astype(BF16)

    centre(es, mb)
    mrelay = start_relays(msent, mbuf, mdiag, msend, mrecv)
    hsent = start_direct(ham.at[0, 0], hbuf, hsend, hrecv)
    wait_direct(msent)
    wait_relayed(mrelay)
    others(es, mbuf, mdiag)

    row = lax.broadcasted_iota(jnp.int32, (N, B), 0)
    col = lax.broadcasted_iota(jnp.int32, (N, B), 1)
    first = jnp.where(row == col, 1.0, 0.0).astype(F32) - es[:, :B].astype(F32)
    e2[:, :N] = dot(es[...], es[...]).astype(BF16)
    e2[:, N:] = first.astype(BF16)
    both = dot(e2[:, :N], e2[...])
    e4[...] = both[:, :N].astype(BF16)
    total = first + both[:, N:]
    term = total.astype(BF16)
    for step in range(3):
        image = dot(e4[...], term)
        total = total + image
        term = image.astype(BF16)
    for p in range(SLOTS):
        xs[p] = total[sl(p), :]

    for c in range(9):
        spot = jnp.int32(SLOTS)
        for p in range(SLOTS):
            spot = jnp.where(live[p] & (cd[p] == c), p, spot)
        wire[c] = xs[spot].astype(BF16)

    zsent, xsent = {}, []
    rows = {"mid": 0, "off": off, "on": on}
    k = 0
    for name, rx in rows.items():
        for far in (1, 0):
            for ay in (1, -1):
                r = rows_of(rx) + 1 + far * ay
                zsent[(name, far, ay)] = remote(
                    wire.at[pl.ds(r, 1)], ibuf.at[pl.ds(9 * code(0, -ay) + r, 1)],
                    isend.at[k], irecv.at[k], (0, ay),
                )
                k += 1

    even_order = (("mid", 1), ("off", 1), ("mid", 0), ("on", 1), ("on", 0), ("off", 0))
    odd_order = (("mid", 1), ("off", 1), ("mid", 0), ("off", 0), ("on", 1), ("on", 0))

    def start_along(order, steps):
        for ay in steps:
            for name, far in order:
                zsent[(name, far, ay)].start()

    for parity, order in ((0, even_order), (1, odd_order)):
        pl.when((core == parity) & (v == 1))(
            functools.partial(start_along, order, (-1, 1))
        )
        pl.when((core == parity) & (v != 1))(
            functools.partial(start_along, order, (1, -1))
        )
    for d, r, n in (
        (off, 4, 1), (off, rows_of(off) + 1, 1), (off, 3, 1), (off, 5, 1),
        (off, rows_of(off), 1), (off, rows_of(off) + 2, 1), (on, 3 * ((on + 1) // 2), 6),
    ):
        copy = remote(
            wire.at[pl.ds(r, n)], ibuf.at[pl.ds(9 * code(-d, 0) + r, n)],
            isend.at[k], irecv.at[k], (d, 0),
        )
        copy.start()
        xsent.append(copy)
        k += 1

    def relay(o, t, r, a, send, recv):
        return remote(
            ibuf.at[pl.ds(9 * code(*o) + r, 1)], ibuf.at[pl.ds(9 * code(*t) + r, 1)],
            isend.at[send], irecv.at[recv], a,
        )

    along_u, along_v, inside = {}, [], {}
    for name in ("mid", "off"):
        for far in (1, 0):
            for w in (1, -1):
                r = rows_of(rows[name]) + 1 - far * w
                along_u[(name, far, w)] = relay((0, w), (-off, w), r, (off, 0), k, k)
                if far == 0:
                    r = 4 if name == "mid" else rows_of(-off) + 1
                    along_v.append(relay((off, 0), (off, w), r, (0, -w), k + 16, k))
                k += 1
    for name in ("mid", "on"):
        for far in (1, 0):
            for w in (1, -1):
                r = rows_of(rows[name]) + 1 - far * w
                inside[(name, far, w)] = relay((0, w), (-on, w), r, (on, 0), k, k)
                k += 1

    def arrived(name, far, then=()):
        for w in (1, -1):
            zsent[(name, far, -w)].wait_recv()
            for copies in then:
                copies[(name, far, w)].start()

    def pass_on(name, far):
        for w in (1, -1):
            inside[(name, far, w)].start()

    def even_relays():
        arrived("mid", 1, (along_u,))
        arrived("off", 1, (along_u,))
        pass_on("mid", 1)
        arrived("mid", 0, (inside,))
        arrived("on", 1, (inside,))
        arrived("on", 0, (inside,))
        arrived("off", 0)
        for copy in xsent[:2]:
            copy.wait_recv()

    def odd_relays():
        arrived("mid", 1, (along_u,))
        for copy in xsent[:2]:
            copy.wait_recv()
        for copy in along_v:
            copy.start()
        arrived("off", 1, (along_u,))
        arrived("mid", 0, (along_u,))
        arrived("off", 0, (along_u,))
        pass_on("mid", 1)
        pass_on("mid", 0)
        arrived("on", 1, (inside,))
        arrived("on", 0, (inside,))

    hrelay = start_relays(hsent, hbuf, hdiag, hsend, hrecv)
    own.wait()
    centre(hs, hown)
    pl.when(core == 0)(even_relays)
    pl.when(core == 1)(odd_relays)

    wait_direct(hsent)
    wait_relayed(hrelay)
    others(hs, hbuf, hdiag)
    wait_sent(msent, mrelay)
    wait_sent(hsent, hrelay)
    for copy in list(zsent.values()) + xsent:
        copy.wait_send()
    for p in range(SLOTS):
        isub[sl(p), sl(0)] = wire[jnp.where(live[p], cd[p], 9)]
    for copy in xsent[2:] + list(along_u.values()) + list(inside.values()):
        copy.wait_recv()
    for q in range(1, SLOTS):
        for p in range(SLOTS):
            ok, r = pair(p, q)
            isub[sl(p), sl(q)] = ibuf[jnp.where(ok, cd[q] * 9 + r, 81)]

    for copy in inside.values():
        copy.wait_send()
    for (name, far, w), copy in along_u.items():
        if far == 1:
            copy.wait_send()
        else:
            pl.when(core == 1)(copy.wait_send)
    for copy in along_v:
        pl.when(core == 1)(copy.wait_send)


def sign_kernel(
    codes_hbm, counts, isub, hs, xs, inv_out, den_out,
    codes, s, h, g, q, ds, sem,
):
    listed = pltpu.make_async_copy(codes_hbm, codes, sem.at[18])
    listed.start()
    ds[SLOTS] = jnp.zeros((B, B), F32)

    product = dot(isub[...], hs[...])
    s[...] = product
    h[...] = product.astype(BF16)
    norm = jnp.sum(jnp.sum(product * product, axis=0, keepdims=True), keepdims=True) / N
    scale = 1.0 / (3.0 * jnp.sqrt(norm) + 1e-6)

    listed.wait()
    count = counts[0, 0]
    spots = []
    for c in range(9):
        at = jnp.int32(SLOTS)
        for p in range(SLOTS):
            at = jnp.where((p < count) & (codes[0, 0, p] == c), p, at)
        spots.append(at)
    inv, blank = [], []
    for c in range(9):
        inv.append(pltpu.make_async_copy(xs.at[spots[c]], inv_out.at[0, 0, c], sem.at[c]))
        blank.append(pltpu.make_async_copy(ds.at[SLOTS], den_out.at[0, 0, c], sem.at[9 + c]))
    for c in range(9):
        inv[c].start()
        pl.when(spots[c] == SLOTS)(blank[c].start)

    a, b = h, g
    for step in range(SIGN - 1):
        square = dot(a[...], a[...])
        q[...] = (square * (scale * scale) if step == 0 else square).astype(BF16)
        new = 1.5 * s[...] - 0.5 * dot(a[...], q[...])
        if step == 0:
            new = new * scale
        s[...] = new
        b[...] = new.astype(BF16)
        a, b = b, a
    q[:, :B] = dot(a[...], a[:, :B]).astype(BF16)
    rows = lax.broadcasted_iota(jnp.int32, (B, B), 0)
    cols = lax.broadcasted_iota(jnp.int32, (B, B), 1)
    ident = jnp.where(rows == cols, 0.5, 0.0).astype(F32)
    image = dot(a[...], q[:, :B])
    for p in range(SLOTS):
        last = 0.25 * image[sl(p), :] - 0.75 * s[sl(p), :B]
        ds[p] = ident + last if p == 0 else last
        c = codes[0, 0, p]
        copy = pltpu.make_async_copy(ds.at[p], den_out.at[0, 0, c], sem.at[9 + c])
        pl.when(p < count)(copy.start)
    for copy in inv + blank:
        copy.wait()


def local(margin_dev, hamiltonian, slot_codes, slot_count):
    vm = pl.BlockSpec(memory_space=pltpu.VMEM)
    hbm = pl.BlockSpec(memory_space=pltpu.HBM)
    shape = jax.ShapeDtypeStruct
    dma = pltpu.SemaphoreType.DMA
    n_sym = 22
    sm = pl.BlockSpec(memory_space=pltpu.SMEM)
    slot_codes, margin_dev, hamiltonian = (
        pltpu.with_memory_space_constraint(x, pltpu.HBM)
        for x in (slot_codes, margin_dev, hamiltonian)
    )
    xs, hs, isub = pl.pallas_call(
        exchange_kernel,
        out_shape=(
            shape((SLOTS + 1, B, B), F32),
            shape((N, N), BF16),
            shape((N, N), BF16),
        ),
        in_specs=[hbm, sm, hbm, hbm],
        out_specs=(vm, vm, vm),
        scratch_shapes=[
            pltpu.SMEM((1, 1, SLOTS), jnp.int32),
            pltpu.VMEM((9, B, B), F32),
            pltpu.VMEM((10, B, B), BF16),
            pltpu.VMEM((82, B, B), BF16),
            pltpu.VMEM((10, B, B), BF16),
            pltpu.VMEM((10, B, B), BF16),
            pltpu.VMEM((82, B, B), BF16),
            pltpu.VMEM((10, B, B), BF16),
            pltpu.VMEM((82, B, B), BF16),
            pltpu.VMEM((10, B, B), BF16),
            pltpu.VMEM((N, N), BF16),
            pltpu.VMEM((N, N + B), BF16),
            pltpu.VMEM((N, N), BF16),
            dma((5,)),
            dma((n_sym,)),
            dma((n_sym,)),
            dma((n_sym,)),
            dma((n_sym,)),
            dma((43,)),
            dma((35,)),
        ],
        compiler_params=pltpu.CompilerParams(
            collective_id=0, has_side_effects=True, vmem_limit_bytes=32 << 20
        ),
        name="exchange",
    )(slot_codes, slot_count, margin_dev, hamiltonian)
    return pl.pallas_call(
        sign_kernel,
        out_shape=(
            shape((1, 1, 9, B, B), F32),
            shape((1, 1, 9, B, B), F32),
        ),
        in_specs=[hbm, sm, vm, vm, vm],
        out_specs=(hbm, hbm),
        scratch_shapes=[
            pltpu.SMEM((1, 1, SLOTS), jnp.int32),
            pltpu.VMEM((N, N), F32),
            pltpu.VMEM((N, N), BF16),
            pltpu.VMEM((N, N), BF16),
            pltpu.VMEM((N, N), BF16),
            pltpu.VMEM((SLOTS + 1, B, B), F32),
            dma((19,)),
        ],
        compiler_params=pltpu.CompilerParams(vmem_limit_bytes=32 << 20),
        name="sign",
    )(slot_codes, slot_count, isub, hs, xs)


def solution(mesh):
    return jax.shard_map(
        local,
        mesh=mesh,
        in_specs=(
            P("gx", "gy", None, None, None),
            P("gx", "gy", None, None, None),
            P("gx", "gy", None),
            P("gx", "gy"),
        ),
        out_specs=(P("gx", "gy", None, None, None), P("gx", "gy", None, None, None)),
        check_vma=False,
    )
```

```python
import functools

import jax
import jax.numpy as jnp
from jax import lax
from jax.experimental import pallas as pl
from jax.experimental.pallas import tpu as pltpu
from jax.sharding import PartitionSpec as P

B = 128
SLOTS = 5
N = SLOTS * B
SIGN = 4
MESH = pl.DeviceIdType.MESH
F32 = jnp.float32
BF16 = jnp.bfloat16
EDGES = ((0, 1), (0, -1), (1, 0), (-1, 0))


def code(dx, dy):
    return 3 * (dx + 1) + dy + 1


def dot(a, b):
    return jnp.dot(a, b, preferred_element_type=F32)


def sl(p):
    return slice(p * B, (p + 1) * B)


def rows_of(step):
    return 3 * (step + 1)


def exchange_kernel(
    codes_hbm, counts, margin, ham,
    xs, hs, isub,
    codes, mf, mb, mbuf, mdiag, hown, hbuf, hdiag, ibuf, wire, es, sq, wd, e2, e4,
    lsem, msend, mrecv, hsend, hrecv, isend, irecv,
):
    nu, nv = lax.axis_size("gx"), lax.axis_size("gy")
    u, v = lax.axis_index("gx"), lax.axis_index("gy")
    core = lax.rem(u, 2)
    off = 2 * core - 1
    on = -off

    def dev(a):
        return (lax.rem(u + a[0] + nu, nu), lax.rem(v + a[1] + nv, nv))

    def remote(src, dst, send, recv, a):
        return pltpu.make_async_remote_copy(
            src_ref=src, dst_ref=dst, send_sem=send, recv_sem=recv,
            device_id=dev(a), device_id_type=MESH,
        )

    barrier = pltpu.get_barrier_semaphore()
    for a in EDGES:
        pl.semaphore_signal(barrier, inc=1, device_id=dev(a), device_id_type=MESH)

    loads = [
        pltpu.make_async_copy(
            margin.at[0, 0, pl.ds(3 * i, 3)], mf.at[pl.ds(3 * i, 3)], lsem.at[i]
        )
        for i in (1, 0, 2)
    ]
    listed = pltpu.make_async_copy(codes_hbm, codes, lsem.at[4])
    own = pltpu.make_async_copy(ham.at[0, 0], hown.at[pl.ds(0, 9)], lsem.at[3])
    for copy in loads + [listed, own]:
        copy.start()

    zero = jnp.zeros((B, B), BF16)
    mb[9] = zero
    hown[9] = zero
    wire[9] = zero
    mbuf[81] = zero
    hbuf[81] = zero
    mdiag[9] = zero
    hdiag[9] = zero
    for g in range(2):
        wd[g, :B, B:] = zero
        wd[g, B:, :B] = zero
    ibuf[81] = zero
    xs[SLOTS] = jnp.zeros((B, B), F32)

    for i, copy in zip((1, 0, 2), loads):
        copy.wait()
        for r in range(3 * i, 3 * i + 3):
            mb[r] = mf[r].astype(BF16)

    pl.semaphore_wait(barrier, 4)

    def start_direct(src, buf, send, recv):
        out = {}
        k = 0
        for r in (4, 7, 1):
            for ay in (1, -1):
                out[(r, ay)] = remote(
                    src.at[pl.ds(r, 1)], buf.at[pl.ds(9 * code(0, -ay) + r, 1)],
                    send.at[k], recv.at[k], (0, ay),
                )
                k += 1
        for name, d in (("off", off), ("on", on)):
            for i, r in enumerate((4, 3, 5, rows_of(d), rows_of(d) + 2)):
                out[(name, i)] = remote(
                    src.at[pl.ds(r, 1)], buf.at[pl.ds(9 * code(-d, 0) + r, 1)],
                    send.at[k], recv.at[k], (d, 0),
                )
                k += 1
        for copy in out.values():
            copy.start()
        return out

    def start_relays(sent, buf, diag, send, recv):
        near, odd, extra = [], [], []
        for j, w in enumerate((1, -1)):
            near.append(remote(
                buf.at[pl.ds(9 * code(0, w) + 4, 1)], diag.at[pl.ds(code(-on, w), 1)],
                send.at[16 + j], recv.at[16 + j], (on, 0),
            ))
            odd.append(remote(
                buf.at[pl.ds(9 * code(0, w) + 4, 1)], diag.at[pl.ds(code(-off, w), 1)],
                send.at[18 + j], recv.at[18 + j], (off, 0),
            ))
            extra.append(remote(
                buf.at[pl.ds(9 * code(off, 0) + 4, 1)], diag.at[pl.ds(code(off, w), 1)],
                send.at[20 + j], recv.at[18 + j], (0, -w),
            ))
        sent[("off", 0)].wait_recv()
        for copy in extra:
            pl.when(core == 1)(copy.start)
        sent[(4, 1)].wait_recv()
        sent[(4, -1)].wait_recv()
        for copy in odd:
            pl.when(core == 1)(copy.start)
        for copy in near:
            copy.start()
        return near, odd, extra

    def wait_direct(sent):
        for key, copy in sent.items():
            if key not in ((4, 1), (4, -1), ("off", 0)):
                copy.wait_recv()

    def wait_relayed(relays):
        for copy in relays[0] + relays[1]:
            copy.wait_recv()

    def wait_sent(sent, relays):
        for copy in list(sent.values()) + relays[0]:
            copy.wait_send()
        for copy in relays[1] + relays[2]:
            pl.when(core == 1)(copy.wait_send)

    msent = start_direct(mb, mbuf, msend, mrecv)

    listed.wait()
    cd = [codes[0, 0, p] for p in range(SLOTS)]
    live = [p < counts[0, 0] for p in range(SLOTS)]
    ox = [c // 3 - 1 for c in cd]
    oy = [c % 3 - 1 for c in cd]

    def pair(p, q):
        rx, ry = ox[p] - ox[q], oy[p] - oy[q]
        ok = (jnp.abs(rx) <= 1) & (jnp.abs(ry) <= 1) & live[p] & live[q]
        return ok, (rx + 1) * 3 + ry + 1

    rank = [jnp.where(ox[p] == 0, 1, jnp.where(oy[p] == 0, 2, 0)) for p in range(SLOTS)]

    def centre(dst, mine):
        for p in range(SLOTS):
            block = mine[jnp.where(live[p], cd[p], 9)]
            dst[sl(p), sl(0)] = block
            if p:
                dst[sl(0), sl(p)] = block.T

    def corner_block(diag, p):
        return diag[jnp.where(live[p] & (rank[p] == 0), cd[p], 9)]

    def others(dst, buf):
        for p in range(1, SLOTS):
            dst[sl(p), sl(p)] = buf[jnp.where(live[p] & (rank[p] > 0), cd[p] * 9 + 4, 81)]
        for p in range(1, SLOTS):
            for q in range(p + 1, SLOTS):
                ok, r = pair(p, q)
                swap = rank[p] > rank[q]
                spot = jnp.where(swap, cd[p] * 9 + 8 - r, cd[q] * 9 + r)
                block = buf[jnp.where(ok, spot, 81)].astype(F32)
                turned = block.T
                flag = jnp.where(swap, 1.0, 0.0).astype(F32)
                keep = 1.0 - flag
                dst[sl(p), sl(q)] = (keep * block + flag * turned).astype(BF16)
                dst[sl(q), sl(p)] = (keep * turned + flag * block).astype(BF16)

    centre(es, mb)
    mrelay = start_relays(msent, mbuf, mdiag, msend, mrecv)
    hsent = start_direct(ham.at[0, 0], hbuf, hsend, hrecv)
    wait_direct(msent)
    others(es, mbuf)

    row = lax.broadcasted_iota(jnp.int32, (N, B), 0)
    col = lax.broadcasted_iota(jnp.int32, (N, B), 1)
    first = jnp.where(row == col, 1.0, 0.0).astype(F32) - es[:, :B].astype(F32)
    e2[:, N:] = first.astype(BF16)
    sq[...] = dot(es[...], es[...])
    wait_relayed(mrelay)
    for p in range(1, SLOTS):
        g, h = divmod(p - 1, 2)
        wd[g, sl(h), sl(h)] = corner_block(mdiag, p)
    groups = (slice(B, 3 * B), slice(3 * B, N))
    right = [dot(es[:, c], wd[g]) for g, c in enumerate(groups)]
    for p in range(1, SLOTS):
        es[sl(p), sl(p)] = es[sl(p), sl(p)] + corner_block(mdiag, p)
    left = [dot(wd[g], es[c, :]) for g, c in enumerate(groups)]
    for r, extra in zip((slice(0, B),) + groups, (None, left[0], left[1])):
        for c, add in zip((slice(0, B),) + groups, (None, right[0], right[1])):
            value = sq[r, c]
            if add is not None:
                value = value + add[r, :]
            if extra is not None:
                value = value + extra[:, c]
            e2[r, c] = value.astype(BF16)
    both = dot(e2[:, :N], e2[...])
    e4[...] = both[:, :N].astype(BF16)
    total = first + both[:, N:]
    term = total.astype(BF16)
    for step in range(3):
        image = dot(e4[...], term)
        total = total + image
        term = image.astype(BF16)
    for p in range(SLOTS):
        xs[p] = total[sl(p), :]

    for c in range(9):
        spot = jnp.int32(SLOTS)
        for p in range(SLOTS):
            spot = jnp.where(live[p] & (cd[p] == c), p, spot)
        wire[c] = xs[spot].astype(BF16)

    zsent, xsent = {}, []
    rows = {"mid": 0, "off": off, "on": on}
    k = 0
    for name, rx in rows.items():
        for far in (1, 0):
            for ay in (1, -1):
                r = rows_of(rx) + 1 + far * ay
                zsent[(name, far, ay)] = remote(
                    wire.at[pl.ds(r, 1)], ibuf.at[pl.ds(9 * code(0, -ay) + r, 1)],
                    isend.at[k], irecv.at[k], (0, ay),
                )
                k += 1

    even_order = (("mid", 1), ("off", 1), ("mid", 0), ("on", 1), ("on", 0), ("off", 0))
    odd_order = (("mid", 1), ("off", 1), ("mid", 0), ("off", 0), ("on", 1), ("on", 0))

    def start_along(order, steps):
        for ay in steps:
            for name, far in order:
                zsent[(name, far, ay)].start()

    for parity, order in ((0, even_order), (1, odd_order)):
        pl.when((core == parity) & (v == 1))(
            functools.partial(start_along, order, (-1, 1))
        )
        pl.when((core == parity) & (v != 1))(
            functools.partial(start_along, order, (1, -1))
        )
    for d, r, n in (
        (off, 4, 1), (off, rows_of(off) + 1, 1), (off, 3, 1), (off, 5, 1),
        (off, rows_of(off), 1), (off, rows_of(off) + 2, 1), (on, 3 * ((on + 1) // 2), 6),
    ):
        copy = remote(
            wire.at[pl.ds(r, n)], ibuf.at[pl.ds(9 * code(-d, 0) + r, n)],
            isend.at[k], irecv.at[k], (d, 0),
        )
        copy.start()
        xsent.append(copy)
        k += 1

    def relay(o, t, r, a, send, recv):
        return remote(
            ibuf.at[pl.ds(9 * code(*o) + r, 1)], ibuf.at[pl.ds(9 * code(*t) + r, 1)],
            isend.at[send], irecv.at[recv], a,
        )

    along_u, along_v, inside = {}, [], {}
    for name in ("mid", "off"):
        for far in (1, 0):
            for w in (1, -1):
                r = rows_of(rows[name]) + 1 - far * w
                along_u[(name, far, w)] = relay((0, w), (-off, w), r, (off, 0), k, k)
                if far == 0:
                    r = 4 if name == "mid" else rows_of(-off) + 1
                    along_v.append(relay((off, 0), (off, w), r, (0, -w), k + 16, k))
                k += 1
    for name in ("mid", "on"):
        for far in (1, 0):
            for w in (1, -1):
                r = rows_of(rows[name]) + 1 - far * w
                inside[(name, far, w)] = relay((0, w), (-on, w), r, (on, 0), k, k)
                k += 1

    def arrived(name, far, then=()):
        for w in (1, -1):
            zsent[(name, far, -w)].wait_recv()
            for copies in then:
                copies[(name, far, w)].start()

    def pass_on(name, far):
        for w in (1, -1):
            inside[(name, far, w)].start()

    def even_relays():
        arrived("mid", 1, (along_u,))
        arrived("off", 1, (along_u,))
        pass_on("mid", 1)
        arrived("mid", 0, (inside,))
        arrived("on", 1, (inside,))
        arrived("on", 0, (inside,))
        arrived("off", 0)
        for copy in xsent[:2]:
            copy.wait_recv()

    def odd_relays():
        arrived("mid", 1, (along_u,))
        for copy in xsent[:2]:
            copy.wait_recv()
        for copy in along_v:
            copy.start()
        arrived("off", 1, (along_u,))
        arrived("mid", 0, (along_u,))
        arrived("off", 0, (along_u,))
        pass_on("mid", 1)
        pass_on("mid", 0)
        arrived("on", 1, (inside,))
        arrived("on", 0, (inside,))

    hrelay = start_relays(hsent, hbuf, hdiag, hsend, hrecv)
    own.wait()
    centre(hs, hown)
    pl.when(core == 0)(even_relays)
    pl.when(core == 1)(odd_relays)

    wait_direct(hsent)
    wait_relayed(hrelay)
    others(hs, hbuf)
    for p in range(1, SLOTS):
        hs[sl(p), sl(p)] = hs[sl(p), sl(p)] + corner_block(hdiag, p)
    wait_sent(msent, mrelay)
    wait_sent(hsent, hrelay)
    for copy in list(zsent.values()) + xsent:
        copy.wait_send()
    for p in range(SLOTS):
        isub[sl(p), sl(0)] = wire[jnp.where(live[p], cd[p], 9)]
    for copy in xsent[2:] + list(along_u.values()) + list(inside.values()):
        copy.wait_recv()
    for q in range(1, SLOTS):
        for p in range(SLOTS):
            ok, r = pair(p, q)
            isub[sl(p), sl(q)] = ibuf[jnp.where(ok, cd[q] * 9 + r, 81)]

    for copy in inside.values():
        copy.wait_send()
    for (name, far, w), copy in along_u.items():
        if far == 1:
            copy.wait_send()
        else:
            pl.when(core == 1)(copy.wait_send)
    for copy in along_v:
        pl.when(core == 1)(copy.wait_send)


def sign_kernel(
    codes_hbm, counts, isub, hs, xs, inv_out, den_out,
    codes, s, h, g, q, ds, sem,
):
    listed = pltpu.make_async_copy(codes_hbm, codes, sem.at[18])
    listed.start()
    ds[SLOTS] = jnp.zeros((B, B), F32)

    product = dot(isub[...], hs[...])
    s[...] = product
    h[...] = product.astype(BF16)
    norm = jnp.sum(jnp.sum(product * product, axis=0, keepdims=True), keepdims=True) / N
    scale = 1.0 / (3.0 * jnp.sqrt(norm) + 1e-6)

    listed.wait()
    count = counts[0, 0]
    spots = []
    for c in range(9):
        at = jnp.int32(SLOTS)
        for p in range(SLOTS):
            at = jnp.where((p < count) & (codes[0, 0, p] == c), p, at)
        spots.append(at)
    inv, blank = [], []
    for c in range(9):
        inv.append(pltpu.make_async_copy(xs.at[spots[c]], inv_out.at[0, 0, c], sem.at[c]))
        blank.append(pltpu.make_async_copy(ds.at[SLOTS], den_out.at[0, 0, c], sem.at[9 + c]))
    for c in range(9):
        inv[c].start()
        pl.when(spots[c] == SLOTS)(blank[c].start)

    a, b = h, g
    for step in range(SIGN - 1):
        square = dot(a[...], a[...])
        q[...] = (square * (scale * scale) if step == 0 else square).astype(BF16)
        new = 1.5 * s[...] - 0.5 * dot(a[...], q[...])
        if step == 0:
            new = new * scale
        s[...] = new
        b[...] = new.astype(BF16)
        a, b = b, a
    q[:, :B] = dot(a[...], a[:, :B]).astype(BF16)
    rows = lax.broadcasted_iota(jnp.int32, (B, B), 0)
    cols = lax.broadcasted_iota(jnp.int32, (B, B), 1)
    ident = jnp.where(rows == cols, 0.5, 0.0).astype(F32)
    image = dot(a[...], q[:, :B])
    for p in range(SLOTS):
        last = 0.25 * image[sl(p), :] - 0.75 * s[sl(p), :B]
        ds[p] = ident + last if p == 0 else last
        c = codes[0, 0, p]
        copy = pltpu.make_async_copy(ds.at[p], den_out.at[0, 0, c], sem.at[9 + c])
        pl.when(p < count)(copy.start)
    for copy in inv + blank:
        copy.wait()


def local(margin_dev, hamiltonian, slot_codes, slot_count):
    vm = pl.BlockSpec(memory_space=pltpu.VMEM)
    hbm = pl.BlockSpec(memory_space=pltpu.HBM)
    shape = jax.ShapeDtypeStruct
    dma = pltpu.SemaphoreType.DMA
    n_sym = 22
    sm = pl.BlockSpec(memory_space=pltpu.SMEM)
    slot_codes, margin_dev, hamiltonian = (
        pltpu.with_memory_space_constraint(x, pltpu.HBM)
        for x in (slot_codes, margin_dev, hamiltonian)
    )
    xs, hs, isub = pl.pallas_call(
        exchange_kernel,
        out_shape=(
            shape((SLOTS + 1, B, B), F32),
            shape((N, N), BF16),
            shape((N, N), BF16),
        ),
        in_specs=[hbm, sm, hbm, hbm],
        out_specs=(vm, vm, vm),
        scratch_shapes=[
            pltpu.SMEM((1, 1, SLOTS), jnp.int32),
            pltpu.VMEM((9, B, B), F32),
            pltpu.VMEM((10, B, B), BF16),
            pltpu.VMEM((82, B, B), BF16),
            pltpu.VMEM((10, B, B), BF16),
            pltpu.VMEM((10, B, B), BF16),
            pltpu.VMEM((82, B, B), BF16),
            pltpu.VMEM((10, B, B), BF16),
            pltpu.VMEM((82, B, B), BF16),
            pltpu.VMEM((10, B, B), BF16),
            pltpu.VMEM((N, N), BF16),
            pltpu.VMEM((N, N), F32),
            pltpu.VMEM((2, 2 * B, 2 * B), BF16),
            pltpu.VMEM((N, N + B), BF16),
            pltpu.VMEM((N, N), BF16),
            dma((5,)),
            dma((n_sym,)),
            dma((n_sym,)),
            dma((n_sym,)),
            dma((n_sym,)),
            dma((43,)),
            dma((35,)),
        ],
        compiler_params=pltpu.CompilerParams(
            collective_id=0, has_side_effects=True, vmem_limit_bytes=32 << 20
        ),
        name="exchange",
    )(slot_codes, slot_count, margin_dev, hamiltonian)
    return pl.pallas_call(
        sign_kernel,
        out_shape=(
            shape((1, 1, 9, B, B), F32),
            shape((1, 1, 9, B, B), F32),
        ),
        in_specs=[hbm, sm, vm, vm, vm],
        out_specs=(hbm, hbm),
        scratch_shapes=[
            pltpu.SMEM((1, 1, SLOTS), jnp.int32),
            pltpu.VMEM((N, N), F32),
            pltpu.VMEM((N, N), BF16),
            pltpu.VMEM((N, N), BF16),
            pltpu.VMEM((N, N), BF16),
            pltpu.VMEM((SLOTS + 1, B, B), F32),
            dma((19,)),
        ],
        compiler_params=pltpu.CompilerParams(vmem_limit_bytes=32 << 20),
        name="sign",
    )(slot_codes, slot_count, isub, hs, xs)


def solution(mesh):
    return jax.shard_map(
        local,
        mesh=mesh,
        in_specs=(
            P("gx", "gy", None, None, None),
            P("gx", "gy", None, None, None),
            P("gx", "gy", None),
            P("gx", "gy"),
        ),
        out_specs=(P("gx", "gy", None, None, None), P("gx", "gy", None, None, None)),
        check_vma=False,
    )
```

```python
import functools

import jax
import jax.numpy as jnp
from jax import lax
from jax.experimental import pallas as pl
from jax.experimental.pallas import tpu as pltpu
from jax.sharding import PartitionSpec as P

B = 128
SLOTS = 5
N = SLOTS * B
SIGN = 4
MESH = pl.DeviceIdType.MESH
F32 = jnp.float32
BF16 = jnp.bfloat16
EDGES = ((0, 1), (0, -1), (1, 0), (-1, 0))


def code(dx, dy):
    return 3 * (dx + 1) + dy + 1


def dot(a, b):
    return jnp.dot(a, b, preferred_element_type=F32)


def sl(p):
    return slice(p * B, (p + 1) * B)


def rows_of(step):
    return 3 * (step + 1)


def exchange_kernel(
    codes_hbm, counts, margin, ham,
    xs, hs, isub,
    codes, mf, mb, mbuf, mdiag, hown, hbuf, hdiag, ibuf, wire, es, e2, e4,
    lsem, msend, mrecv, hsend, hrecv, isend, irecv,
):
    nu, nv = lax.axis_size("gx"), lax.axis_size("gy")
    u, v = lax.axis_index("gx"), lax.axis_index("gy")
    core = lax.rem(u, 2)
    off = 2 * core - 1
    on = -off

    def dev(a):
        return (lax.rem(u + a[0] + nu, nu), lax.rem(v + a[1] + nv, nv))

    def remote(src, dst, send, recv, a):
        return pltpu.make_async_remote_copy(
            src_ref=src, dst_ref=dst, send_sem=send, recv_sem=recv,
            device_id=dev(a), device_id_type=MESH,
        )

    barrier = pltpu.get_barrier_semaphore()
    for a in EDGES:
        pl.semaphore_signal(barrier, inc=1, device_id=dev(a), device_id_type=MESH)

    loads = [
        pltpu.make_async_copy(
            margin.at[0, 0, pl.ds(3 * i, 3)], mf.at[pl.ds(3 * i, 3)], lsem.at[i]
        )
        for i in (1, 0, 2)
    ]
    listed = pltpu.make_async_copy(codes_hbm, codes, lsem.at[4])
    own = pltpu.make_async_copy(ham.at[0, 0], hown.at[pl.ds(0, 9)], lsem.at[3])
    for copy in loads + [listed, own]:
        copy.start()

    zero = jnp.zeros((B, B), BF16)
    mb[9] = zero
    hown[9] = zero
    wire[9] = zero
    mbuf[81] = zero
    hbuf[81] = zero
    mdiag[9] = zero
    hdiag[9] = zero
    ibuf[81] = zero
    xs[SLOTS] = jnp.zeros((B, B), F32)

    for i, copy in zip((1, 0, 2), loads):
        copy.wait()
        for r in range(3 * i, 3 * i + 3):
            mb[r] = mf[r].astype(BF16)

    pl.semaphore_wait(barrier, 4)

    def start_direct(src, buf, send, recv):
        out = {}
        k = 0
        for r in (4, 7, 1):
            for ay in (1, -1):
                out[(r, ay)] = remote(
                    src.at[pl.ds(r, 1)], buf.at[pl.ds(9 * code(0, -ay) + r, 1)],
                    send.at[k], recv.at[k], (0, ay),
                )
                k += 1
        for name, d in (("off", off), ("on", on)):
            for i, r in enumerate((4, 3, 5, rows_of(d), rows_of(d) + 2)):
                out[(name, i)] = remote(
                    src.at[pl.ds(r, 1)], buf.at[pl.ds(9 * code(-d, 0) + r, 1)],
                    send.at[k], recv.at[k], (d, 0),
                )
                k += 1
        for copy in out.values():
            copy.start()
        return out

    def start_relays(sent, buf, diag, send, recv):
        near, odd, extra = [], [], []
        for j, w in enumerate((1, -1)):
            near.append(remote(
                buf.at[pl.ds(9 * code(0, w) + 4, 1)], diag.at[pl.ds(code(-on, w), 1)],
                send.at[16 + j], recv.at[16 + j], (on, 0),
            ))
            odd.append(remote(
                buf.at[pl.ds(9 * code(0, w) + 4, 1)], diag.at[pl.ds(code(-off, w), 1)],
                send.at[18 + j], recv.at[18 + j], (off, 0),
            ))
            extra.append(remote(
                buf.at[pl.ds(9 * code(off, 0) + 4, 1)], diag.at[pl.ds(code(off, w), 1)],
                send.at[20 + j], recv.at[18 + j], (0, -w),
            ))
        sent[("off", 0)].wait_recv()
        for copy in extra:
            pl.when(core == 1)(copy.start)
        sent[(4, 1)].wait_recv()
        sent[(4, -1)].wait_recv()
        for copy in odd:
            pl.when(core == 1)(copy.start)
        for copy in near:
            copy.start()
        return near, odd, extra

    def wait_direct(sent):
        for key, copy in sent.items():
            if key not in ((4, 1), (4, -1), ("off", 0)):
                copy.wait_recv()

    def wait_relayed(relays):
        for copy in relays[0] + relays[1]:
            copy.wait_recv()

    def wait_sent(sent, relays):
        for copy in list(sent.values()) + relays[0]:
            copy.wait_send()
        for copy in relays[1] + relays[2]:
            pl.when(core == 1)(copy.wait_send)

    msent = start_direct(mb, mbuf, msend, mrecv)

    listed.wait()
    cd = [codes[0, 0, p] for p in range(SLOTS)]
    live = [p < counts[0, 0] for p in range(SLOTS)]
    ox = [c // 3 - 1 for c in cd]
    oy = [c % 3 - 1 for c in cd]

    def pair(p, q):
        rx, ry = ox[p] - ox[q], oy[p] - oy[q]
        ok = (jnp.abs(rx) <= 1) & (jnp.abs(ry) <= 1) & live[p] & live[q]
        return ok, (rx + 1) * 3 + ry + 1

    rank = [jnp.where(ox[p] == 0, 1, jnp.where(oy[p] == 0, 2, 0)) for p in range(SLOTS)]

    def centre(dst, mine):
        for p in range(SLOTS):
            block = mine[jnp.where(live[p], cd[p], 9)]
            dst[sl(p), sl(0)] = block
            if p:
                dst[sl(0), sl(p)] = block.T

    def others(dst, buf, diag):
        for p in range(1, SLOTS):
            edge = rank[p] > 0
            block = buf[jnp.where(live[p] & edge, cd[p] * 9 + 4, 81)]
            far = diag[jnp.where(live[p] & jnp.logical_not(edge), cd[p], 9)]
            dst[sl(p), sl(p)] = block + far
        for p in range(1, SLOTS):
            for q in range(p + 1, SLOTS):
                ok, r = pair(p, q)
                swap = rank[p] > rank[q]
                spot = jnp.where(swap, cd[p] * 9 + 8 - r, cd[q] * 9 + r)
                block = buf[jnp.where(ok, spot, 81)].astype(F32)
                turned = block.T
                flag = jnp.where(swap, 1.0, 0.0).astype(F32)
                keep = 1.0 - flag
                dst[sl(p), sl(q)] = (keep * block + flag * turned).astype(BF16)
                dst[sl(q), sl(p)] = (keep * turned + flag * block).astype(BF16)

    centre(es, mb)
    mrelay = start_relays(msent, mbuf, mdiag, msend, mrecv)
    hsent = start_direct(ham.at[0, 0], hbuf, hsend, hrecv)
    wait_direct(msent)
    wait_relayed(mrelay)
    others(es, mbuf, mdiag)

    row = lax.broadcasted_iota(jnp.int32, (N, B), 0)
    col = lax.broadcasted_iota(jnp.int32, (N, B), 1)
    first = jnp.where(row == col, 1.0, 0.0).astype(F32) - es[:, :B].astype(F32)
    e2[:, :N] = dot(es[...], es[...]).astype(BF16)
    e2[:, N:] = first.astype(BF16)
    both = dot(e2[:, :N], e2[...])
    e4[...] = both[:, :N].astype(BF16)
    total = first + both[:, N:]
    term = total.astype(BF16)
    for step in range(3):
        image = dot(e4[...], term)
        total = total + image
        term = image.astype(BF16)
    for p in range(SLOTS):
        xs[p] = total[sl(p), :]

    for c in range(9):
        spot = jnp.int32(SLOTS)
        for p in range(SLOTS):
            spot = jnp.where(live[p] & (cd[p] == c), p, spot)
        wire[c] = xs[spot].astype(BF16)

    zsent, xsent = {}, []
    rows = {"mid": 0, "off": off, "on": on}
    k = 0
    for name, rx in rows.items():
        for far in (1, 0):
            for ay in (1, -1):
                r = rows_of(rx) + 1 + far * ay
                zsent[(name, far, ay)] = remote(
                    wire.at[pl.ds(r, 1)], ibuf.at[pl.ds(9 * code(0, -ay) + r, 1)],
                    isend.at[k], irecv.at[k], (0, ay),
                )
                k += 1

    even_order = (("mid", 1), ("off", 1), ("mid", 0), ("on", 1), ("on", 0), ("off", 0))
    odd_order = (("mid", 1), ("off", 1), ("mid", 0), ("off", 0), ("on", 1), ("on", 0))

    def start_along(order, steps):
        for ay in steps:
            for name, far in order:
                zsent[(name, far, ay)].start()

    for d, r, n in (
        (off, 4, 1), (off, rows_of(off) + 1, 1), (off, 3, 1), (off, 5, 1),
        (off, rows_of(off), 1), (off, rows_of(off) + 2, 1), (on, 3 * ((on + 1) // 2), 6),
    ):
        copy = remote(
            wire.at[pl.ds(r, n)], ibuf.at[pl.ds(9 * code(-d, 0) + r, n)],
            isend.at[k], irecv.at[k], (d, 0),
        )
        xsent.append(copy)
        k += 1
    for copy in xsent[:2]:
        copy.start()
    for parity, order in ((0, even_order), (1, odd_order)):
        pl.when((core == parity) & (v == 1))(
            functools.partial(start_along, order, (-1, 1))
        )
        pl.when((core == parity) & (v != 1))(
            functools.partial(start_along, order, (1, -1))
        )
    for copy in xsent[2:]:
        copy.start()

    def relay(o, t, r, a, send, recv):
        return remote(
            ibuf.at[pl.ds(9 * code(*o) + r, 1)], ibuf.at[pl.ds(9 * code(*t) + r, 1)],
            isend.at[send], irecv.at[recv], a,
        )

    along_u, along_v, inside = {}, [], {}
    for name in ("mid", "off"):
        for far in (1, 0):
            for w in (1, -1):
                r = rows_of(rows[name]) + 1 - far * w
                along_u[(name, far, w)] = relay((0, w), (-off, w), r, (off, 0), k, k)
                if far == 0:
                    r = 4 if name == "mid" else rows_of(-off) + 1
                    along_v.append(relay((off, 0), (off, w), r, (0, -w), k + 16, k))
                k += 1
    for name in ("mid", "on"):
        for far in (1, 0):
            for w in (1, -1):
                r = rows_of(rows[name]) + 1 - far * w
                inside[(name, far, w)] = relay((0, w), (-on, w), r, (on, 0), k, k)
                k += 1

    def arrived(name, far, then=()):
        for w in (1, -1):
            zsent[(name, far, -w)].wait_recv()
            for copies in then:
                copies[(name, far, w)].start()

    def pass_on(name, far):
        for w in (1, -1):
            inside[(name, far, w)].start()

    def even_relays():
        arrived("mid", 1, (along_u,))
        arrived("off", 1, (along_u,))
        pass_on("mid", 1)
        arrived("mid", 0, (inside,))
        arrived("on", 1, (inside,))
        arrived("on", 0, (inside,))
        arrived("off", 0)
        for copy in xsent[:2]:
            copy.wait_recv()

    def odd_relays():
        arrived("mid", 1, (along_u,))
        for copy in xsent[:2]:
            copy.wait_recv()
        for copy in along_v:
            copy.start()
        arrived("off", 1, (along_u,))
        arrived("mid", 0, (along_u,))
        arrived("off", 0, (along_u,))
        pass_on("mid", 1)
        pass_on("mid", 0)
        arrived("on", 1, (inside,))
        arrived("on", 0, (inside,))

    hrelay = start_relays(hsent, hbuf, hdiag, hsend, hrecv)
    own.wait()
    centre(hs, hown)
    pl.when(core == 0)(even_relays)
    pl.when(core == 1)(odd_relays)

    wait_direct(hsent)
    wait_relayed(hrelay)
    others(hs, hbuf, hdiag)
    wait_sent(msent, mrelay)
    wait_sent(hsent, hrelay)
    for copy in list(zsent.values()) + xsent:
        copy.wait_send()
    for p in range(SLOTS):
        isub[sl(p), sl(0)] = wire[jnp.where(live[p], cd[p], 9)]
    for copy in xsent[2:] + list(along_u.values()) + list(inside.values()):
        copy.wait_recv()
    for q in range(1, SLOTS):
        for p in range(SLOTS):
            ok, r = pair(p, q)
            isub[sl(p), sl(q)] = ibuf[jnp.where(ok, cd[q] * 9 + r, 81)]

    for copy in inside.values():
        copy.wait_send()
    for (name, far, w), copy in along_u.items():
        if far == 1:
            copy.wait_send()
        else:
            pl.when(core == 1)(copy.wait_send)
    for copy in along_v:
        pl.when(core == 1)(copy.wait_send)


def sign_kernel(
    codes_hbm, counts, isub, hs, xs, inv_out, den_out,
    codes, s, h, g, q, ds, sem,
):
    listed = pltpu.make_async_copy(codes_hbm, codes, sem.at[18])
    listed.start()
    ds[SLOTS] = jnp.zeros((B, B), F32)

    product = dot(isub[...], hs[...])
    s[...] = product
    h[...] = product.astype(BF16)
    norm = jnp.sum(jnp.sum(product * product, axis=0, keepdims=True), keepdims=True) / N
    scale = 1.0 / (3.0 * jnp.sqrt(norm) + 1e-6)

    listed.wait()
    count = counts[0, 0]
    spots = []
    for c in range(9):
        at = jnp.int32(SLOTS)
        for p in range(SLOTS):
            at = jnp.where((p < count) & (codes[0, 0, p] == c), p, at)
        spots.append(at)
    inv, blank = [], []
    for c in range(9):
        inv.append(pltpu.make_async_copy(xs.at[spots[c]], inv_out.at[0, 0, c], sem.at[c]))
        blank.append(pltpu.make_async_copy(ds.at[SLOTS], den_out.at[0, 0, c], sem.at[9 + c]))
    for c in range(9):
        inv[c].start()
        pl.when(spots[c] == SLOTS)(blank[c].start)

    a, b = h, g
    for step in range(SIGN - 1):
        square = dot(a[...], a[...])
        q[...] = (square * (scale * scale) if step == 0 else square).astype(BF16)
        new = 1.5 * s[...] - 0.5 * dot(a[...], q[...])
        if step == 0:
            new = new * scale
        s[...] = new
        b[...] = new.astype(BF16)
        a, b = b, a
    q[:, :B] = dot(a[...], a[:, :B]).astype(BF16)
    rows = lax.broadcasted_iota(jnp.int32, (B, B), 0)
    cols = lax.broadcasted_iota(jnp.int32, (B, B), 1)
    ident = jnp.where(rows == cols, 0.5, 0.0).astype(F32)
    image = dot(a[...], q[:, :B])
    for p in range(SLOTS):
        last = 0.25 * image[sl(p), :] - 0.75 * s[sl(p), :B]
        ds[p] = ident + last if p == 0 else last
        c = codes[0, 0, p]
        copy = pltpu.make_async_copy(ds.at[p], den_out.at[0, 0, c], sem.at[9 + c])
        pl.when(p < count)(copy.start)
    for copy in inv + blank:
        copy.wait()


def local(margin_dev, hamiltonian, slot_codes, slot_count):
    vm = pl.BlockSpec(memory_space=pltpu.VMEM)
    hbm = pl.BlockSpec(memory_space=pltpu.HBM)
    shape = jax.ShapeDtypeStruct
    dma = pltpu.SemaphoreType.DMA
    n_sym = 22
    sm = pl.BlockSpec(memory_space=pltpu.SMEM)
    slot_codes, margin_dev, hamiltonian = (
        pltpu.with_memory_space_constraint(x, pltpu.HBM)
        for x in (slot_codes, margin_dev, hamiltonian)
    )
    xs, hs, isub = pl.pallas_call(
        exchange_kernel,
        out_shape=(
            shape((SLOTS + 1, B, B), F32),
            shape((N, N), BF16),
            shape((N, N), BF16),
        ),
        in_specs=[hbm, sm, hbm, hbm],
        out_specs=(vm, vm, vm),
        scratch_shapes=[
            pltpu.SMEM((1, 1, SLOTS), jnp.int32),
            pltpu.VMEM((9, B, B), F32),
            pltpu.VMEM((10, B, B), BF16),
            pltpu.VMEM((82, B, B), BF16),
            pltpu.VMEM((10, B, B), BF16),
            pltpu.VMEM((10, B, B), BF16),
            pltpu.VMEM((82, B, B), BF16),
            pltpu.VMEM((10, B, B), BF16),
            pltpu.VMEM((82, B, B), BF16),
            pltpu.VMEM((10, B, B), BF16),
            pltpu.VMEM((N, N), BF16),
            pltpu.VMEM((N, N + B), BF16),
            pltpu.VMEM((N, N), BF16),
            dma((5,)),
            dma((n_sym,)),
            dma((n_sym,)),
            dma((n_sym,)),
            dma((n_sym,)),
            dma((43,)),
            dma((35,)),
        ],
        compiler_params=pltpu.CompilerParams(
            collective_id=0, has_side_effects=True, vmem_limit_bytes=32 << 20
        ),
        name="exchange",
    )(slot_codes, slot_count, margin_dev, hamiltonian)
    return pl.pallas_call(
        sign_kernel,
        out_shape=(
            shape((1, 1, 9, B, B), F32),
            shape((1, 1, 9, B, B), F32),
        ),
        in_specs=[hbm, sm, vm, vm, vm],
        out_specs=(hbm, hbm),
        scratch_shapes=[
            pltpu.SMEM((1, 1, SLOTS), jnp.int32),
            pltpu.VMEM((N, N), F32),
            pltpu.VMEM((N, N), BF16),
            pltpu.VMEM((N, N), BF16),
            pltpu.VMEM((N, N), BF16),
            pltpu.VMEM((SLOTS + 1, B, B), F32),
            dma((19,)),
        ],
        compiler_params=pltpu.CompilerParams(vmem_limit_bytes=32 << 20),
        name="sign",
    )(slot_codes, slot_count, isub, hs, xs)


def solution(mesh):
    return jax.shard_map(
        local,
        mesh=mesh,
        in_specs=(
            P("gx", "gy", None, None, None),
            P("gx", "gy", None, None, None),
            P("gx", "gy", None),
            P("gx", "gy"),
        ),
        out_specs=(P("gx", "gy", None, None, None), P("gx", "gy", None, None, None)),
        check_vma=False,
    )
```

```python
import functools

import jax
import jax.numpy as jnp
from jax import lax
from jax.experimental import pallas as pl
from jax.experimental.pallas import tpu as pltpu
from jax.sharding import PartitionSpec as P

B = 128
SLOTS = 5
N = SLOTS * B
SIGN = 4
MESH = pl.DeviceIdType.MESH
F32 = jnp.float32
BF16 = jnp.bfloat16
EDGES = ((0, 1), (0, -1), (1, 0), (-1, 0))


def code(dx, dy):
    return 3 * (dx + 1) + dy + 1


def dot(a, b):
    return jnp.dot(a, b, preferred_element_type=F32)


def sl(p):
    return slice(p * B, (p + 1) * B)


def rows_of(step):
    return 3 * (step + 1)


def exchange_kernel(
    codes_hbm, counts, margin, ham,
    xs, hs, isub,
    codes, mf, mb, mbuf, mdiag, hown, hbuf, hdiag, ibuf, wire, es, e2, e4,
    lsem, msend, mrecv, hsend, hrecv, isend, irecv,
):
    nu, nv = lax.axis_size("gx"), lax.axis_size("gy")
    u, v = lax.axis_index("gx"), lax.axis_index("gy")
    core = lax.rem(u, 2)
    off = 2 * core - 1
    on = -off

    def dev(a):
        return (lax.rem(u + a[0] + nu, nu), lax.rem(v + a[1] + nv, nv))

    def remote(src, dst, send, recv, a):
        return pltpu.make_async_remote_copy(
            src_ref=src, dst_ref=dst, send_sem=send, recv_sem=recv,
            device_id=dev(a), device_id_type=MESH,
        )

    barrier = pltpu.get_barrier_semaphore()
    for a in EDGES:
        pl.semaphore_signal(barrier, inc=1, device_id=dev(a), device_id_type=MESH)

    loads = [
        pltpu.make_async_copy(
            margin.at[0, 0, pl.ds(3 * i, 3)], mf.at[pl.ds(3 * i, 3)], lsem.at[i]
        )
        for i in (1, 0, 2)
    ]
    listed = pltpu.make_async_copy(codes_hbm, codes, lsem.at[4])
    own = pltpu.make_async_copy(ham.at[0, 0], hown.at[pl.ds(0, 9)], lsem.at[3])
    for copy in loads + [listed, own]:
        copy.start()

    zero = jnp.zeros((B, B), BF16)
    mb[9] = zero
    hown[9] = zero
    wire[9] = zero
    mbuf[81] = zero
    hbuf[81] = zero
    mdiag[9] = zero
    hdiag[9] = zero
    ibuf[81] = zero
    xs[SLOTS] = jnp.zeros((B, B), F32)

    for i, copy in zip((1, 0, 2), loads):
        copy.wait()
        for r in range(3 * i, 3 * i + 3):
            mb[r] = mf[r].astype(BF16)

    pl.semaphore_wait(barrier, 4)

    def start_direct(src, buf, send, recv):
        out = {}
        k = 0
        for r in (4, 7, 1):
            for ay in (1, -1):
                out[(r, ay)] = remote(
                    src.at[pl.ds(r, 1)], buf.at[pl.ds(9 * code(0, -ay) + r, 1)],
                    send.at[k], recv.at[k], (0, ay),
                )
                k += 1
        for name, d in (("off", off), ("on", on)):
            for i, r in enumerate((4, 3, 5, rows_of(d), rows_of(d) + 2)):
                out[(name, i)] = remote(
                    src.at[pl.ds(r, 1)], buf.at[pl.ds(9 * code(-d, 0) + r, 1)],
                    send.at[k], recv.at[k], (d, 0),
                )
                k += 1
        for copy in out.values():
            copy.start()
        return out

    def start_relays(sent, buf, diag, send, recv):
        near, odd, extra = [], [], []
        for j, w in enumerate((1, -1)):
            near.append(remote(
                buf.at[pl.ds(9 * code(0, w) + 4, 1)], diag.at[pl.ds(code(-on, w), 1)],
                send.at[16 + j], recv.at[16 + j], (on, 0),
            ))
            odd.append(remote(
                buf.at[pl.ds(9 * code(0, w) + 4, 1)], diag.at[pl.ds(code(-off, w), 1)],
                send.at[18 + j], recv.at[18 + j], (off, 0),
            ))
            extra.append(remote(
                buf.at[pl.ds(9 * code(off, 0) + 4, 1)], diag.at[pl.ds(code(off, w), 1)],
                send.at[20 + j], recv.at[18 + j], (0, -w),
            ))
        sent[("off", 0)].wait_recv()
        for copy in extra:
            pl.when(core == 1)(copy.start)
        sent[(4, 1)].wait_recv()
        sent[(4, -1)].wait_recv()
        for copy in odd:
            pl.when(core == 1)(copy.start)
        for copy in near:
            copy.start()
        return near, odd, extra

    def wait_direct(sent):
        for key, copy in sent.items():
            if key not in ((4, 1), (4, -1), ("off", 0)):
                copy.wait_recv()

    def wait_relayed(relays):
        for copy in relays[0] + relays[1]:
            copy.wait_recv()

    def wait_sent(sent, relays):
        for copy in list(sent.values()) + relays[0]:
            copy.wait_send()
        for copy in relays[1] + relays[2]:
            pl.when(core == 1)(copy.wait_send)

    msent = start_direct(mb, mbuf, msend, mrecv)

    listed.wait()
    cd = [codes[0, 0, p] for p in range(SLOTS)]
    live = [p < counts[0, 0] for p in range(SLOTS)]
    ox = [c // 3 - 1 for c in cd]
    oy = [c % 3 - 1 for c in cd]

    def pair(p, q):
        rx, ry = ox[p] - ox[q], oy[p] - oy[q]
        ok = (jnp.abs(rx) <= 1) & (jnp.abs(ry) <= 1) & live[p] & live[q]
        return ok, (rx + 1) * 3 + ry + 1

    rank = [jnp.where(ox[p] == 0, 1, jnp.where(oy[p] == 0, 2, 0)) for p in range(SLOTS)]

    def centre(dst, mine):
        for p in range(SLOTS):
            block = mine[jnp.where(live[p], cd[p], 9)]
            dst[sl(p), sl(0)] = block
            if p:
                dst[sl(0), sl(p)] = block.T

    def others(dst, buf, diag):
        for p in range(1, SLOTS):
            edge = rank[p] > 0
            block = buf[jnp.where(live[p] & edge, cd[p] * 9 + 4, 81)]
            far = diag[jnp.where(live[p] & jnp.logical_not(edge), cd[p], 9)]
            dst[sl(p), sl(p)] = block + far
        for p in range(1, SLOTS):
            for q in range(p + 1, SLOTS):
                ok, r = pair(p, q)
                swap = rank[p] > rank[q]
                spot = jnp.where(swap, cd[p] * 9 + 8 - r, cd[q] * 9 + r)
                block = buf[jnp.where(ok, spot, 81)].astype(F32)
                turned = block.T
                flag = jnp.where(swap, 1.0, 0.0).astype(F32)
                keep = 1.0 - flag
                dst[sl(p), sl(q)] = (keep * block + flag * turned).astype(BF16)
                dst[sl(q), sl(p)] = (keep * turned + flag * block).astype(BF16)

    centre(es, mb)
    mrelay = start_relays(msent, mbuf, mdiag, msend, mrecv)
    hsent = start_direct(ham.at[0, 0], hbuf, hsend, hrecv)
    wait_direct(msent)
    wait_relayed(mrelay)
    others(es, mbuf, mdiag)

    row = lax.broadcasted_iota(jnp.int32, (N, B), 0)
    col = lax.broadcasted_iota(jnp.int32, (N, B), 1)
    first = jnp.where(row == col, 1.0, 0.0).astype(F32) - es[:, :B].astype(F32)
    e2[:, :N] = dot(es[...], es[...]).astype(BF16)
    e2[:, N:] = first.astype(BF16)
    both = dot(e2[:, :N], e2[...])
    e4[...] = both[:, :N].astype(BF16)
    total = first + both[:, N:]
    term = total.astype(BF16)
    for step in range(3):
        image = dot(e4[...], term)
        total = total + image
        term = image.astype(BF16)
    for p in range(SLOTS):
        xs[p] = total[sl(p), :]

    for c in range(9):
        spot = jnp.int32(SLOTS)
        for p in range(SLOTS):
            spot = jnp.where(live[p] & (cd[p] == c), p, spot)
        wire[c] = xs[spot].astype(BF16)

    zsent, xsent = {}, []
    rows = {"mid": 0, "off": off, "on": on}
    k = 0
    for name, rx in rows.items():
        for far in (1, 0):
            for ay in (1, -1):
                r = rows_of(rx) + 1 + far * ay
                zsent[(name, far, ay)] = remote(
                    wire.at[pl.ds(r, 1)], ibuf.at[pl.ds(9 * code(0, -ay) + r, 1)],
                    isend.at[k], irecv.at[k], (0, ay),
                )
                k += 1

    even_order = (("mid", 1), ("off", 1), ("mid", 0), ("on", 1), ("on", 0), ("off", 0))
    odd_order = (("mid", 1), ("off", 1), ("mid", 0), ("off", 0), ("on", 1), ("on", 0))

    def start_along(order, steps):
        for ay in steps:
            for name, far in order:
                zsent[(name, far, ay)].start()

    for d, r, n in (
        (off, 4, 1), (off, rows_of(off) + 1, 1), (off, 3, 1), (off, 5, 1),
        (off, rows_of(off), 1), (off, rows_of(off) + 2, 1), (on, 3 * ((on + 1) // 2), 6),
    ):
        copy = remote(
            wire.at[pl.ds(r, n)], ibuf.at[pl.ds(9 * code(-d, 0) + r, n)],
            isend.at[k], irecv.at[k], (d, 0),
        )
        xsent.append(copy)
        k += 1
    for copy in xsent[:6]:
        copy.start()
    for parity, order in ((0, even_order), (1, odd_order)):
        pl.when((core == parity) & (v == 1))(
            functools.partial(start_along, order, (-1, 1))
        )
        pl.when((core == parity) & (v != 1))(
            functools.partial(start_along, order, (1, -1))
        )
    for copy in xsent[6:]:
        copy.start()

    def relay(o, t, r, a, send, recv):
        return remote(
            ibuf.at[pl.ds(9 * code(*o) + r, 1)], ibuf.at[pl.ds(9 * code(*t) + r, 1)],
            isend.at[send], irecv.at[recv], a,
        )

    along_u, along_v, inside = {}, [], {}
    for name in ("mid", "off"):
        for far in (1, 0):
            for w in (1, -1):
                r = rows_of(rows[name]) + 1 - far * w
                along_u[(name, far, w)] = relay((0, w), (-off, w), r, (off, 0), k, k)
                if far == 0:
                    r = 4 if name == "mid" else rows_of(-off) + 1
                    along_v.append(relay((off, 0), (off, w), r, (0, -w), k + 16, k))
                k += 1
    for name in ("mid", "on"):
        for far in (1, 0):
            for w in (1, -1):
                r = rows_of(rows[name]) + 1 - far * w
                inside[(name, far, w)] = relay((0, w), (-on, w), r, (on, 0), k, k)
                k += 1

    def arrived(name, far, then=()):
        for w in (1, -1):
            zsent[(name, far, -w)].wait_recv()
            for copies in then:
                copies[(name, far, w)].start()

    def pass_on(name, far):
        for w in (1, -1):
            inside[(name, far, w)].start()

    def even_relays():
        arrived("mid", 1, (along_u,))
        arrived("off", 1, (along_u,))
        pass_on("mid", 1)
        arrived("mid", 0, (inside,))
        arrived("on", 1, (inside,))
        arrived("on", 0, (inside,))
        arrived("off", 0)
        for copy in xsent[:2]:
            copy.wait_recv()

    def odd_relays():
        arrived("mid", 1, (along_u,))
        for copy in xsent[:2]:
            copy.wait_recv()
        for copy in along_v:
            copy.start()
        arrived("off", 1, (along_u,))
        arrived("mid", 0, (along_u,))
        arrived("off", 0, (along_u,))
        pass_on("mid", 1)
        pass_on("mid", 0)
        arrived("on", 1, (inside,))
        arrived("on", 0, (inside,))

    hrelay = start_relays(hsent, hbuf, hdiag, hsend, hrecv)
    own.wait()
    centre(hs, hown)
    pl.when(core == 0)(even_relays)
    pl.when(core == 1)(odd_relays)

    wait_direct(hsent)
    wait_relayed(hrelay)
    others(hs, hbuf, hdiag)
    wait_sent(msent, mrelay)
    wait_sent(hsent, hrelay)
    for copy in list(zsent.values()) + xsent:
        copy.wait_send()
    for p in range(SLOTS):
        isub[sl(p), sl(0)] = wire[jnp.where(live[p], cd[p], 9)]
    for copy in xsent[2:] + list(along_u.values()) + list(inside.values()):
        copy.wait_recv()
    for q in range(1, SLOTS):
        for p in range(SLOTS):
            ok, r = pair(p, q)
            isub[sl(p), sl(q)] = ibuf[jnp.where(ok, cd[q] * 9 + r, 81)]

    for copy in inside.values():
        copy.wait_send()
    for (name, far, w), copy in along_u.items():
        if far == 1:
            copy.wait_send()
        else:
            pl.when(core == 1)(copy.wait_send)
    for copy in along_v:
        pl.when(core == 1)(copy.wait_send)


def sign_kernel(
    codes_hbm, counts, isub, hs, xs, inv_out, den_out,
    codes, s, h, g, q, ds, sem,
):
    listed = pltpu.make_async_copy(codes_hbm, codes, sem.at[18])
    listed.start()
    ds[SLOTS] = jnp.zeros((B, B), F32)

    product = dot(isub[...], hs[...])
    s[...] = product
    h[...] = product.astype(BF16)
    norm = jnp.sum(jnp.sum(product * product, axis=0, keepdims=True), keepdims=True) / N
    scale = 1.0 / (3.0 * jnp.sqrt(norm) + 1e-6)

    listed.wait()
    count = counts[0, 0]
    spots = []
    for c in range(9):
        at = jnp.int32(SLOTS)
        for p in range(SLOTS):
            at = jnp.where((p < count) & (codes[0, 0, p] == c), p, at)
        spots.append(at)
    inv, blank = [], []
    for c in range(9):
        inv.append(pltpu.make_async_copy(xs.at[spots[c]], inv_out.at[0, 0, c], sem.at[c]))
        blank.append(pltpu.make_async_copy(ds.at[SLOTS], den_out.at[0, 0, c], sem.at[9 + c]))
    for c in range(9):
        inv[c].start()
        pl.when(spots[c] == SLOTS)(blank[c].start)

    a, b = h, g
    for step in range(SIGN - 1):
        square = dot(a[...], a[...])
        q[...] = (square * (scale * scale) if step == 0 else square).astype(BF16)
        new = 1.5 * s[...] - 0.5 * dot(a[...], q[...])
        if step == 0:
            new = new * scale
        s[...] = new
        b[...] = new.astype(BF16)
        a, b = b, a
    q[:, :B] = dot(a[...], a[:, :B]).astype(BF16)
    rows = lax.broadcasted_iota(jnp.int32, (B, B), 0)
    cols = lax.broadcasted_iota(jnp.int32, (B, B), 1)
    ident = jnp.where(rows == cols, 0.5, 0.0).astype(F32)
    image = dot(a[...], q[:, :B])
    for p in range(SLOTS):
        last = 0.25 * image[sl(p), :] - 0.75 * s[sl(p), :B]
        ds[p] = ident + last if p == 0 else last
        c = codes[0, 0, p]
        copy = pltpu.make_async_copy(ds.at[p], den_out.at[0, 0, c], sem.at[9 + c])
        pl.when(p < count)(copy.start)
    for copy in inv + blank:
        copy.wait()


def local(margin_dev, hamiltonian, slot_codes, slot_count):
    vm = pl.BlockSpec(memory_space=pltpu.VMEM)
    hbm = pl.BlockSpec(memory_space=pltpu.HBM)
    shape = jax.ShapeDtypeStruct
    dma = pltpu.SemaphoreType.DMA
    n_sym = 22
    sm = pl.BlockSpec(memory_space=pltpu.SMEM)
    slot_codes, margin_dev, hamiltonian = (
        pltpu.with_memory_space_constraint(x, pltpu.HBM)
        for x in (slot_codes, margin_dev, hamiltonian)
    )
    xs, hs, isub = pl.pallas_call(
        exchange_kernel,
        out_shape=(
            shape((SLOTS + 1, B, B), F32),
            shape((N, N), BF16),
            shape((N, N), BF16),
        ),
        in_specs=[hbm, sm, hbm, hbm],
        out_specs=(vm, vm, vm),
        scratch_shapes=[
            pltpu.SMEM((1, 1, SLOTS), jnp.int32),
            pltpu.VMEM((9, B, B), F32),
            pltpu.VMEM((10, B, B), BF16),
            pltpu.VMEM((82, B, B), BF16),
            pltpu.VMEM((10, B, B), BF16),
            pltpu.VMEM((10, B, B), BF16),
            pltpu.VMEM((82, B, B), BF16),
            pltpu.VMEM((10, B, B), BF16),
            pltpu.VMEM((82, B, B), BF16),
            pltpu.VMEM((10, B, B), BF16),
            pltpu.VMEM((N, N), BF16),
            pltpu.VMEM((N, N + B), BF16),
            pltpu.VMEM((N, N), BF16),
            dma((5,)),
            dma((n_sym,)),
            dma((n_sym,)),
            dma((n_sym,)),
            dma((n_sym,)),
            dma((43,)),
            dma((35,)),
        ],
        compiler_params=pltpu.CompilerParams(
            collective_id=0, has_side_effects=True, vmem_limit_bytes=32 << 20
        ),
        name="exchange",
    )(slot_codes, slot_count, margin_dev, hamiltonian)
    return pl.pallas_call(
        sign_kernel,
        out_shape=(
            shape((1, 1, 9, B, B), F32),
            shape((1, 1, 9, B, B), F32),
        ),
        in_specs=[hbm, sm, vm, vm, vm],
        out_specs=(hbm, hbm),
        scratch_shapes=[
            pltpu.SMEM((1, 1, SLOTS), jnp.int32),
            pltpu.VMEM((N, N), F32),
            pltpu.VMEM((N, N), BF16),
            pltpu.VMEM((N, N), BF16),
            pltpu.VMEM((N, N), BF16),
            pltpu.VMEM((SLOTS + 1, B, B), F32),
            dma((19,)),
        ],
        compiler_params=pltpu.CompilerParams(vmem_limit_bytes=32 << 20),
        name="sign",
    )(slot_codes, slot_count, isub, hs, xs)


def solution(mesh):
    return jax.shard_map(
        local,
        mesh=mesh,
        in_specs=(
            P("gx", "gy", None, None, None),
            P("gx", "gy", None, None, None),
            P("gx", "gy", None),
            P("gx", "gy"),
        ),
        out_specs=(P("gx", "gy", None, None, None), P("gx", "gy", None, None, None)),
        check_vma=False,
    )
```
